1024 devices in a mesh: group: 4 (over x), tile: 256 (over z, y, core).
Axes of the slice: x: 4, y: 8, z: 16, core: 2. Of those that a mesh axis runs over, the one named last changes fastest.
Arguments:
- facies: int32 [256, 2048, 256], P('group', 'tile'), may hold values from 0 to 7
- perm_table: float32 [8], replicated, may hold values from 0.05 to 10
- source: float32 [256, 2048, 256], P('group', 'tile'), may hold values from -6 to 6
Outputs:
- head: float32 [256, 2048, 256], P('group', 'tile')
The draws below stay inside these ranges and needn't reach their ends.
All inputs are finite; a program needn't handle non-finite values.
Results may differ from the reference program's by a relative error of at most 0.0003.
Values sent between devices are 32-bit elements; how exact they have to be, the bound alone decides.
No kernel may reach another device: no remote copies, remote signals or barrier semaphores. Data moves between devices by JAX's collectives and lax.ppermute only.
A program may use at most 32 MiB of HBM per device.

```python
import math
import jax
import jax.numpy as jnp
from jax import lax

CX = 64
CY = 8
CZ = 256
NF = 8
COARSE_ITERS = 3
NX = 256
NY = 2048
N_GROUP = 4
N_TILE = 256


def draw_facies(key, part):
    key_plane, key_low, key_high = jax.random.split(jax.random.fold_in(key, 11), 3)
    plane_kind = jax.random.randint(key_plane, (NX, 1, 1), 0, 3)
    low_kind = jax.random.randint(key_low, (NX, NY, CZ), 0, 2)
    high_kind = jax.random.randint(key_high, (NX, NY, CZ), 2, NF)
    return jnp.where(plane_kind == 0, high_kind, low_kind).astype(jnp.int32)


def draw_perm_table(key, part):
    key_low, key_high = jax.random.split(jax.random.fold_in(key, 7))
    u_low = jax.random.uniform(key_low, (NF,), jnp.float32)
    u_high = jax.random.uniform(key_high, (NF,), jnp.float32)
    low_perm = 0.05 * jnp.exp(u_low * math.log(2.0))
    high_perm = 2.0 * jnp.exp(u_high * math.log(5.0))
    return jnp.where(jnp.arange(NF) < 2, low_perm, high_perm).astype(jnp.float32)


def block_levels(rng, dims, cuts, least, largest):
    gain = 1.0
    for position, parts in cuts:
        draws = jax.random.uniform(jax.random.fold_in(jax.random.fold_in(rng, 6), position), (parts,), jnp.float32, least / len(cuts), largest / len(cuts))
        gain = gain * jnp.repeat(jnp.exp(draws), dims[position] // parts).reshape((-1,) + (1,) * (len(dims) - 1 - position))
    return gain


def normal_values(rng, dims, scale, bound, pieces=(), dtype=jnp.bfloat16):
    loudness = block_levels(rng, dims, pieces, -0.22, 0.18) if pieces else 1.0
    result = jax.random.normal(rng, dims, jnp.float32) * scale * loudness
    return jnp.minimum(jnp.maximum(result, -bound), bound).astype(dtype)


def setup_inputs(seed: int = 0) -> dict:
    arg_keys = jax.random.split(jax.random.key(seed), 4)
    facies = draw_facies(jax.random.fold_in(arg_keys[3], 71), 0)
    perm_table = draw_perm_table(jax.random.fold_in(arg_keys[3], 71), 0)
    source = normal_values(arg_keys[2], (NX, NY, CZ), 1.0, 6.0, ((0, 4), (1, 256)), jnp.float32)
    return {"facies": facies, "perm_table": perm_table, "source": source}


relax_weight = 0.8

def harmonic(left_perm, right_perm):
    pair_sum = left_perm + right_perm
    positive = pair_sum > 0.0
    return jnp.where(positive, 2.0 * left_perm * right_perm / jnp.where(positive, pair_sum, 1.0), 0.0)

def operator(head_ext, perm_ext, storage):
    perm_mid = perm_ext[1:-1, 1:-1]
    head_mid = head_ext[1:-1, 1:-1]
    flux_sum = storage * head_mid
    diagonal = storage + jnp.zeros_like(head_mid)
    pairs = [(perm_ext[2:, 1:-1], head_ext[2:, 1:-1]), (perm_ext[:-2, 1:-1], head_ext[:-2, 1:-1]), (perm_ext[1:-1, 2:], head_ext[1:-1, 2:]), (perm_ext[1:-1, :-2], head_ext[1:-1, :-2])]
    perm_z = jnp.pad(perm_mid, ((0, 0), (0, 0), (1, 1)))
    head_z = jnp.pad(head_mid, ((0, 0), (0, 0), (1, 1)))
    pairs = pairs + [(perm_z[:, :, 2:], head_z[:, :, 2:]), (perm_z[:, :, :-2], head_z[:, :, :-2])]
    for perm_nb, head_nb in pairs:
        trans = harmonic(perm_mid, perm_nb)
        flux_sum = flux_sum + trans * (head_mid - head_nb)
        diagonal = diagonal + trans
    return (flux_sum, diagonal)

def sweep(head_ext, perm_ext, rhs_mid, storage):
    flux_sum, diagonal = operator(head_ext, perm_ext, storage)
    return head_ext[1:-1, 1:-1] + relax_weight * (rhs_mid - flux_sum) / diagonal

def coarse_solve(coarse_rhs, link_x, link_y, store_brick):
    zero_row = jnp.zeros_like(coarse_rhs[:1])
    zero_col = jnp.zeros_like(coarse_rhs[:, :1])
    link_x_prev = jnp.concatenate([zero_row, link_x[:-1]], axis=0)
    link_y_prev = jnp.concatenate([zero_col, link_y[:, :-1]], axis=1)
    diagonal = store_brick + link_x + link_x_prev + link_y + link_y_prev
    lower = -link_y_prev
    upper = -link_y
    correction = jnp.zeros_like(coarse_rhs)
    for sweep_no in range(COARSE_ITERS):
        before = jnp.concatenate([zero_row, correction[:-1]], axis=0)
        after = jnp.concatenate([correction[1:], zero_row], axis=0)
        rhs_now = coarse_rhs + link_x_prev * before + link_x * after
        correction = lax.linalg.tridiagonal_solve(lower, diagonal, upper, rhs_now[..., None])[..., 0]
    return correction

def pad_plane(field):
    return jnp.pad(field, ((1, 1), (1, 1), (0, 0)))

def reference(facies, perm_table, source):
    storage = 0.01 / CY
    perm = perm_table[facies]
    perm_pad = pad_plane(perm)
    head_zero = jnp.zeros(perm_pad.shape, jnp.float32)
    head_one = sweep(head_zero, perm_pad, source, storage)
    head_two = sweep(pad_plane(head_one), perm_pad, source, storage)
    flux_sum, unused = operator(pad_plane(head_two), perm_pad, storage)
    resid = source - flux_sum
    coarse_rhs = resid.reshape(N_GROUP, CX, N_TILE, CY, CZ).sum(axis=(1, 3, 4))
    last_x = perm[CX - 1::CX]
    next_x = jnp.concatenate([perm[CX::CX], jnp.zeros_like(perm[:1])], axis=0)
    link_x = harmonic(last_x, next_x).sum(axis=2).reshape(N_GROUP, N_TILE, CY).sum(axis=2)
    last_y = perm[:, CY - 1::CY]
    next_y = jnp.concatenate([perm[:, CY::CY], jnp.zeros_like(perm[:, :1])], axis=1)
    link_y = harmonic(last_y, next_y).sum(axis=2).reshape(N_GROUP, CX, N_TILE).sum(axis=1)
    correction = coarse_solve(coarse_rhs, link_x, link_y, storage * CX * CY * CZ)
    spread = jnp.repeat(jnp.repeat(correction, CX, axis=0), CY, axis=1)
    head_three = head_two + spread[:, :, None]
    head_four = sweep(pad_plane(head_three), perm_pad, source, storage)
    return sweep(pad_plane(head_four), perm_pad, source, storage)
```

```python
import functools

import jax
import jax.numpy as jnp
from jax import lax
from jax.experimental import pallas as pl
from jax.experimental.pallas import tpu as pltpu
from jax.sharding import Mesh
from jax.sharding import PartitionSpec as P

COARSE_ITERS = 3
RELAX = 0.8
HALO = 4
TILE_AXES = ("z", "y", "core")
ROWS = 16
VMEM = pl.BlockSpec(memory_space=pltpu.VMEM)
SMEM = pl.BlockSpec(memory_space=pltpu.SMEM)


def position():
    z, y, core = (lax.axis_index(a) for a in TILE_AXES)
    tile = (z * lax.axis_size("y") + y) * lax.axis_size("core") + core
    return lax.axis_index("group"), tile, core, y


def call(kernel, out_shape, in_specs, scratch=(), name=None, cost=None):
    outs = jax.tree.map(lambda _: VMEM, out_shape)
    return pl.pallas_call(
        kernel,
        out_shape=out_shape,
        in_specs=in_specs,
        out_specs=outs,
        scratch_shapes=list(scratch),
        name=name,
        cost_estimate=cost,
        compiler_params=pltpu.CompilerParams(vmem_limit_bytes=48 * 1024 * 1024),
    )


def f32(*shape):
    return jax.ShapeDtypeStruct(shape, jnp.float32)


def rows_kernel(table_ref, facies_ref, source_ref, r_ref, near_ref, far_ref):
    core = position()[2]
    planes, rows, depth = facies_ref.shape
    low = lax.broadcasted_iota(jnp.int32, (rows, depth), 0) < rows // 2
    kinds = table_ref.shape[0]
    first = core == 0

    def body(x, carry):
        facies = facies_ref[x]
        perm = jnp.full((rows, depth), table_ref[0], jnp.float32)
        for kind in range(1, kinds):
            perm = jnp.where(facies == kind, table_ref[kind], perm)
        r = 1.0 / perm
        source = source_ref[x]
        r_ref[x] = r
        begin = jnp.where(low, r, pltpu.roll(source, rows // 2, 0))
        end = jnp.where(low, pltpu.roll(r, rows // 2, 0), source)
        near_ref[x] = jnp.where(first, end, begin)
        far_ref[x] = jnp.where(first, begin, end)
        return carry

    lax.fori_loop(0, planes, body, 0, unroll=4)


def halo_rows(near_ref, far_ref, x, core, tile, tiles):
    rows = far_ref.shape[1]
    depth = far_ref.shape[2]
    low = lax.broadcasted_iota(jnp.int32, (rows, depth), 0) < rows // 2
    near = near_ref[1 - core, x]
    far = far_ref[x]
    first = core == 0
    after = jnp.where(first, near, far)
    before = jnp.where(first, far, near)
    r = jnp.where(low, after, pltpu.roll(before, rows // 2, 0))
    source = jnp.where(low, pltpu.roll(after, rows // 2, 0), before)
    absent = (low & (tile == tiles - 1)) | (~low & (tile == 0))
    return jnp.where(absent, 1.0, r), jnp.where(absent, 0.0, source)


def planes_kernel(r_ref, source_ref, near_ref, far_ref, begin_ref, end_ref):
    _, tile, core, _ = position()
    tiles = lax.axis_size("z") * lax.axis_size("y") * lax.axis_size("core")
    planes = r_ref.shape[0]
    for d in range(HALO):
        for out, x in ((begin_ref, d), (end_ref, planes - 1 - d)):
            out[d] = r_ref[x]
            if d < HALO - 1:
                side_r, side_source = halo_rows(near_ref, far_ref, x, core, tile, tiles)
                out[4 + d] = side_r
                out[7 + d] = source_ref[x]
                if d < HALO - 2:
                    out[10 + d] = side_source


def fine_kernel(
    storage,
    r_ref, source_ref, near_ref, far_ref, begin_ref, end_ref,
    sums_ref, v_ref, tx_ref, ty_ref, tz_ref, w_ref, ws_ref,
    rr_ref, ss_ref, h_ref,
):
    group, tile, core, y_pos = position()
    groups = lax.axis_size("group")
    tiles = lax.axis_size("z") * lax.axis_size("y") * lax.axis_size("core")
    planes, rows, depth = r_ref.shape
    wide = planes + 2 * HALO
    ones = jnp.ones((rows, depth), jnp.float32)
    zeros = jnp.zeros((rows, depth), jnp.float32)
    for d in range(HALO):
        for recv, x, there in (
            (end_ref, HALO - 1 - d, group > 0),
            (begin_ref, HALO + planes + d, group < groups - 1),
        ):
            rr_ref[x, 0:rows] = jnp.where(there, recv[d], 1.0)
            rr_ref[x, rows:ROWS] = jnp.where(there, recv[4 + d], 1.0) if d < HALO - 1 else ones
            ss_ref[x, 0:rows] = jnp.where(there, recv[7 + d], 0.0) if d < HALO - 1 else zeros
            ss_ref[x, rows:ROWS] = jnp.where(there, recv[10 + d], 0.0) if d < HALO - 2 else zeros

    def gather_rows(x, carry):
        side_r, side_source = halo_rows(near_ref, far_ref, x, core, tile, tiles)
        rr_ref[HALO + x, 0:rows] = r_ref[x]
        rr_ref[HALO + x, rows:ROWS] = side_r
        ss_ref[HALO + x, 0:rows] = source_ref[x]
        ss_ref[HALO + x, rows:ROWS] = side_source
        return carry

    lax.fori_loop(0, planes, gather_rows, 0, unroll=2)

    row = lax.broadcasted_iota(jnp.int32, (ROWS, depth), 0)
    column = lax.broadcasted_iota(jnp.int32, (ROWS, depth), 1)
    y_wall = ((row == ROWS - 1) & (tile == 0)) | ((row == rows - 1) & (tile == tiles - 1))
    z_wall = column == depth - 1

    def faces(x, before):
        r = rr_ref[x]
        x_wall = ((x == HALO - 1) & (group == 0)) | ((x == HALO + planes - 1) & (group == groups - 1))
        tx = jnp.where(x_wall, 0.0, 2.0 / (r + rr_ref[x + 1]))
        ty = jnp.where(y_wall, 0.0, 2.0 / (r + pltpu.roll(r, ROWS - 1, 0)))
        tz = jnp.where(z_wall, 0.0, 2.0 / (r + pltpu.roll(r, depth - 1, 1)))
        diagonal = storage + tx + before + ty + pltpu.roll(ty, 1, 0) + tz + pltpu.roll(tz, 1, 1)
        w = RELAX / diagonal
        ws = w * ss_ref[x]
        tx_ref[x] = tx
        ty_ref[x] = ty
        tz_ref[x] = tz
        w_ref[x] = w
        ws_ref[x] = ws
        h_ref[x] = ws
        return tx

    start = 2.0 / (rr_ref[0] + rr_ref[1])
    lax.fori_loop(1, wide - 1, faces, start, unroll=2)

    def second(x, carry):
        total, y_flux, before = carry
        h = h_ref[x]
        tx = tx_ref[x]
        v, ahead = relax(h, h_ref[x + 1], before, tx, ty_ref[x], tz_ref[x], w_ref[x], ws_ref[x], depth)
        v_ref[x] = v
        inside = (x >= HALO) & (x < HALO + planes)
        total = total + jnp.where(inside, ss_ref[x, 0:rows] - storage * v[0:rows], 0.0)
        flux = ty_ref[x] * (v - pltpu.roll(v, ROWS - 1, 0))
        y_flux = y_flux + jnp.where(inside, flux, 0.0)
        return total, y_flux, ahead

    wide_zeros = jnp.zeros((ROWS, depth), jnp.float32)
    first_flow = tx_ref[1] * h_ref[1]
    total, y_flux, _ = lax.fori_loop(
        2, wide - 2, second, (zeros, wide_zeros, first_flow), unroll=2
    )
    left, right = HALO - 1, HALO + planes - 1
    out_left = tx_ref[left, 0:rows] * (v_ref[left + 1, 0:rows] - v_ref[left, 0:rows])
    out_right = tx_ref[right, 0:rows] * (v_ref[right, 0:rows] - v_ref[right + 1, 0:rows])
    side = jnp.where(row == ROWS - 1, y_flux, jnp.where(row == rows - 1, -y_flux, 0.0))
    rhs = total - out_left - out_right + side[0:rows] + side[rows:ROWS]
    rhs = jnp.sum(rhs, keepdims=True)
    link_x = jnp.sum(tx_ref[right, 0:rows], keepdims=True)

    def y_links(x, acc):
        return acc + ty_ref[HALO + x, 0:rows]

    link_y = lax.fori_loop(0, planes, y_links, zeros, unroll=8)
    link_y = jnp.sum(jnp.where(row[0:rows] == rows - 1, link_y, 0.0), keepdims=True)
    lane = lax.broadcasted_iota(jnp.int32, (8, 128), 1) - 8 * group
    mine = lax.broadcasted_iota(jnp.int32, (8, 128), 0) == y_pos
    packed = jnp.where(lane == 0, rhs, 0.0) + jnp.where(lane == 1, link_x, 0.0)
    packed = jnp.where(mine, packed + jnp.where(lane == 2, link_y, 0.0), 0.0)
    for peer in range(sums_ref.shape[0]):
        sums_ref[peer] = packed


def relax(h, h_next, before, tx, ty, tz, w, ws, depth):
    ahead = tx * h
    flow = before + tx * h_next
    flow = flow + ty * pltpu.roll(h, h.shape[0] - 1, 0) + pltpu.roll(ty * h, 1, 0)
    flow = flow + tz * pltpu.roll(h, depth - 1, 1) + pltpu.roll(tz * h, 1, 1)
    return (1.0 - RELAX) * h + ws + w * flow, ahead


def merge_kernel(part_ref, out_ref):
    total = part_ref[0]
    for peer in range(1, part_ref.shape[0]):
        total = total + part_ref[peer]
    for peer in range(out_ref.shape[0]):
        out_ref[peer] = total


def before_by(pair, stride):
    even, odd = pair
    length = even.shape[0]
    if stride == 1:
        return pltpu.roll(odd, 1, 0), even
    shift = stride // 2
    return pltpu.roll(even, shift, 0), pltpu.roll(odd, shift, 0)


def after_by(pair, stride):
    even, odd = pair
    length = even.shape[0]
    if stride == 1:
        return odd, pltpu.roll(even, length - 1, 0)
    shift = length - stride // 2
    return pltpu.roll(even, shift, 0), pltpu.roll(odd, shift, 0)


def each(fn, *pairs):
    return tuple(fn(*values) for values in zip(*pairs, strict=True))


def coarse_solve(sums_ref, store_brick, levels):
    lines = sums_ref.shape[0] // 2
    rhs = tuple(
        jnp.concatenate([sums_ref[2 * z + core] for z in range(lines)], axis=0) for core in range(2)
    )
    lanes = rhs[0].shape[1]
    link_x = each(lambda a: pltpu.roll(a, lanes - 1, 1), rhs)
    link_y = each(lambda a: pltpu.roll(a, lanes - 2, 1), rhs)
    link_x_before = each(lambda a: pltpu.roll(a, 8, 1), link_x)
    link_y_before = before_by(link_y, 1)
    diagonal = each(lambda a, b, c, d: store_brick + a + b + c + d, link_x, link_x_before, link_y, link_y_before)
    upper = each(lambda a: -a, link_y)
    alphas, gammas = [], []
    for level in range(levels):
        stride = 1 << level
        inverse = each(lambda d: 1.0 / d, diagonal)
        ratio = each(lambda u, i: -u * i, upper, inverse)
        alpha = before_by(ratio, stride)
        gamma = each(lambda u, i: -u * i, upper, after_by(inverse, stride))
        low = before_by(each(lambda q, u: q * u, ratio, upper), stride)
        diagonal = each(lambda d, a, g, u: d + a + g * u, diagonal, low, gamma, upper)
        upper = each(lambda g, u: g * u, gamma, after_by(upper, stride))
        alphas.append(alpha)
        gammas.append(gamma)
    inverse = each(lambda d: 1.0 / d, diagonal)
    correction = None
    for sweep_no in range(COARSE_ITERS):
        now = rhs
        if sweep_no:
            now = each(
                lambda r, a, b, c: r + a * pltpu.roll(c, 8, 1) + b * pltpu.roll(c, lanes - 8, 1),
                rhs, link_x_before, link_x, correction,
            )
        for level in range(levels):
            stride = 1 << level
            now = each(
                lambda n, a, p, g, q: n + a * p + g * q,
                now, alphas[level], before_by(now, stride), gammas[level], after_by(now, stride),
            )
        correction = each(lambda n, i: n * i, now, inverse)
    return correction


def last_kernel(
    store_brick, levels,
    sums_ref, v_ref, tx_ref, ty_ref, tz_ref, w_ref, ws_ref,
    out_ref,
    lines_ref, h_ref, g_ref,
):
    group, tile, core, _ = position()
    planes, rows, depth = out_ref.shape
    even, odd = coarse_solve(sums_ref, store_brick, levels)
    length = even.shape[0]
    for parity, line in ((0, even), (1, odd)):
        lines_ref[parity, 0:8] = jnp.zeros((8, line.shape[1]), jnp.float32)
        lines_ref[parity, 8 : 8 + length] = line
        lines_ref[parity, 8 + length : 16 + length] = jnp.zeros((8, line.shape[1]), jnp.float32)
    half = tile // 2
    here = lines_ref[core, pl.ds(8 + half, 1), :]
    ahead = lines_ref[1 - core, pl.ds(8 + half + core, 1), :]
    behind = lines_ref[1 - core, pl.ds(7 + half + core, 1), :]
    lane = lax.broadcasted_iota(jnp.int32, here.shape, 1)
    row = lax.broadcasted_iota(jnp.int32, (ROWS, depth), 0)

    def shift_of(offset):
        own, up, down = (
            jnp.sum(jnp.where(lane == 8 * (group + offset), line, 0.0), keepdims=True)
            for line in (here, ahead, behind)
        )
        return jnp.where(row < rows, own, jnp.where(row < rows + HALO, up, down))

    shifts = [shift_of(offset) for offset in (-1, 0, 1)]
    for x in (2, 3):
        h_ref[x] = v_ref[x] + shifts[0]
        h_ref[HALO + planes + x - 2] = v_ref[HALO + planes + x - 2] + shifts[2]
    middle = shifts[1]

    def lift(x, carry):
        h_ref[x] = v_ref[x] + middle
        return carry

    lax.fori_loop(HALO, HALO + planes, lift, 0, unroll=4)

    def third(x, before):
        v, ahead = relax(
            h_ref[x], h_ref[x + 1], before, tx_ref[x], ty_ref[x], tz_ref[x], w_ref[x], ws_ref[x], depth
        )
        g_ref[x] = v
        return ahead

    lax.fori_loop(HALO - 1, HALO + planes + 1, third, tx_ref[HALO - 2] * h_ref[HALO - 2], unroll=2)

    def fourth(x, before):
        h = g_ref[x]
        h_own = h[0:rows]
        tx = tx_ref[x, 0:rows]
        tz = tz_ref[x, 0:rows]
        ty = ty_ref[x]
        ahead = tx * h_own
        flow = before + tx * g_ref[x + 1, 0:rows]
        flow = flow + (ty * pltpu.roll(h, ROWS - 1, 0) + pltpu.roll(ty * h, 1, 0))[0:rows]
        flow = flow + tz * pltpu.roll(h_own, depth - 1, 1) + pltpu.roll(tz * h_own, 1, 1)
        out_ref[x - HALO] = (1.0 - RELAX) * h_own + ws_ref[x, 0:rows] + w_ref[x, 0:rows] * flow
        return ahead

    first = tx_ref[HALO - 1, 0:rows] * g_ref[HALO - 1, 0:rows]
    lax.fori_loop(HALO, HALO + planes, fourth, first, unroll=2)


def spread(block, axes):
    return lax.all_to_all(block, axes, 0, 0)


def on_device(facies, perm_table, source):
    planes, rows, depth = source.shape
    storage = 0.01 / rows
    groups = lax.axis_size("group")
    z_size, y_size, cores = (lax.axis_size(a) for a in TILE_AXES)
    tiles = z_size * y_size * cores
    brick = f32(planes, rows, depth)
    r, near, far = call(rows_kernel, (brick, brick, brick), [SMEM, VMEM, VMEM], name="rows")(
        perm_table, facies, source
    )
    pairs = [p for i in range(1, tiles - 1, 2) for p in ((i, i + 1), (i + 1, i))]
    far = lax.ppermute(far, TILE_AXES, pairs)
    near = lax.all_gather(near, "core")
    slab = f32(12, rows, depth)
    begin, end = call(planes_kernel, (slab, slab), [VMEM] * 4, name="planes")(r, source, near, far)
    end = lax.ppermute(end, "group", [(i, i + 1) for i in range(groups - 1)])
    begin = lax.ppermute(begin, "group", [(i + 1, i) for i in range(groups - 1)])
    wide = f32(planes + 2 * HALO, ROWS, depth)
    scratch = [pltpu.VMEM(wide.shape, jnp.float32)]
    sums, *fields = call(
        functools.partial(fine_kernel, storage),
        (f32(groups * y_size, 8, 128),) + (wide,) * 6,
        [VMEM] * 6,
        scratch * 3,
        name="fine",
    )(r, source, near, far, begin, end)
    sums = spread(sums, ("group", "y"))
    sums = call(merge_kernel, f32(z_size * cores, 8, 128), [VMEM], name="merge")(sums)
    sums = spread(sums, ("z", "core"))
    length = z_size * y_size
    return call(
        functools.partial(last_kernel, storage * planes * rows * depth, tiles.bit_length() - 1),
        brick,
        [VMEM] * 7,
        [pltpu.VMEM((2, length + 16, 128), jnp.float32)] + scratch * 2,
        name="last",
    )(sums, *fields)


def solution(mesh):
    groups, tiles = mesh.shape["group"], mesh.shape["tile"]
    chips = Mesh(mesh.devices.reshape(groups, tiles // 16, 8, 2), ("group",) + TILE_AXES)
    cells = P("group", TILE_AXES, None)
    return jax.shard_map(
        on_device, mesh=chips, in_specs=(cells, P(), cells), out_specs=cells, check_vma=False
    )
```

```python
import functools

import jax
import jax.numpy as jnp
from jax import lax
from jax.experimental import pallas as pl
from jax.experimental.pallas import tpu as pltpu
from jax.sharding import Mesh
from jax.sharding import PartitionSpec as P

COARSE_ITERS = 3
RELAX = 0.8
HALO = 4
TILE_AXES = ("z", "y", "core")
ROWS = 16
VMEM = pl.BlockSpec(memory_space=pltpu.VMEM)
SMEM = pl.BlockSpec(memory_space=pltpu.SMEM)


def position():
    z, y, core = (lax.axis_index(a) for a in TILE_AXES)
    tile = (z * lax.axis_size("y") + y) * lax.axis_size("core") + core
    return lax.axis_index("group"), tile, core, y


def call(kernel, out_shape, in_specs, scratch=(), name=None, cost=None):
    outs = jax.tree.map(lambda _: VMEM, out_shape)
    return pl.pallas_call(
        kernel,
        out_shape=out_shape,
        in_specs=in_specs,
        out_specs=outs,
        scratch_shapes=list(scratch),
        name=name,
        cost_estimate=cost,
        compiler_params=pltpu.CompilerParams(vmem_limit_bytes=24 * 1024 * 1024),
    )


def f32(*shape):
    return jax.ShapeDtypeStruct(shape, jnp.float32)


def rows_kernel(table_ref, facies_ref, source_ref, r_ref, near_ref, far_ref):
    core = position()[2]
    planes, rows, depth = facies_ref.shape
    low = lax.broadcasted_iota(jnp.int32, (rows, depth), 0) < rows // 2
    kinds = table_ref.shape[0]
    first = core == 0

    def body(x, carry):
        facies = facies_ref[x]
        perm = jnp.full((rows, depth), table_ref[0], jnp.float32)
        for kind in range(1, kinds):
            perm = jnp.where(facies == kind, table_ref[kind], perm)
        r = 1.0 / perm
        source = source_ref[x]
        r_ref[x] = r
        begin = jnp.where(low, r, pltpu.roll(source, rows // 2, 0))
        end = jnp.where(low, pltpu.roll(r, rows // 2, 0), source)
        near_ref[x] = jnp.where(first, end, begin)
        far_ref[x] = jnp.where(first, begin, end)
        return carry

    lax.fori_loop(0, planes, body, 0, unroll=4)


def halo_rows(near_ref, far_ref, x, core, tile, tiles):
    rows = far_ref.shape[1]
    depth = far_ref.shape[2]
    low = lax.broadcasted_iota(jnp.int32, (rows, depth), 0) < rows // 2
    near = near_ref[x]
    far = far_ref[x]
    first = core == 0
    after = jnp.where(first, near, far)
    before = jnp.where(first, far, near)
    r = jnp.where(low, after, pltpu.roll(before, rows // 2, 0))
    source = jnp.where(low, pltpu.roll(after, rows // 2, 0), before)
    absent = (low & (tile == tiles - 1)) | (~low & (tile == 0))
    return jnp.where(absent, 1.0, r), jnp.where(absent, 0.0, source)


def planes_kernel(r_ref, source_ref, near_ref, far_ref, begin_ref, end_ref):
    _, tile, core, _ = position()
    tiles = lax.axis_size("z") * lax.axis_size("y") * lax.axis_size("core")
    planes = r_ref.shape[0]
    for d in range(HALO):
        for out, x in ((begin_ref, d), (end_ref, planes - 1 - d)):
            out[d] = r_ref[x]
            if d < HALO - 1:
                side_r, side_source = halo_rows(near_ref, far_ref, x, core, tile, tiles)
                out[4 + d] = side_r
                out[7 + d] = source_ref[x]
                if d < HALO - 2:
                    out[10 + d] = side_source


def fine_kernel(
    storage,
    r_ref, source_ref, near_ref, far_ref, begin_ref, end_ref,
    sums_ref, v_ref, tx_ref, ty_ref, tz_ref, w_ref, ws_ref,
    rr_ref, ss_ref, h_ref,
):
    group, tile, core, y_pos = position()
    groups = lax.axis_size("group")
    tiles = lax.axis_size("z") * lax.axis_size("y") * lax.axis_size("core")
    planes, rows, depth = r_ref.shape
    wide = planes + 2 * HALO
    ones = jnp.ones((rows, depth), jnp.float32)
    zeros = jnp.zeros((rows, depth), jnp.float32)
    for d in range(HALO):
        for recv, x, there in (
            (end_ref, HALO - 1 - d, group > 0),
            (begin_ref, HALO + planes + d, group < groups - 1),
        ):
            rr_ref[x, 0:rows] = jnp.where(there, recv[d], 1.0)
            rr_ref[x, rows:ROWS] = jnp.where(there, recv[4 + d], 1.0) if d < HALO - 1 else ones
            ss_ref[x, 0:rows] = jnp.where(there, recv[7 + d], 0.0) if d < HALO - 1 else zeros
            ss_ref[x, rows:ROWS] = jnp.where(there, recv[10 + d], 0.0) if d < HALO - 2 else zeros

    def gather_rows(x, carry):
        side_r, side_source = halo_rows(near_ref, far_ref, x, core, tile, tiles)
        rr_ref[HALO + x, 0:rows] = r_ref[x]
        rr_ref[HALO + x, rows:ROWS] = side_r
        ss_ref[HALO + x, 0:rows] = source_ref[x]
        ss_ref[HALO + x, rows:ROWS] = side_source
        return carry

    lax.fori_loop(0, planes, gather_rows, 0, unroll=2)

    row = lax.broadcasted_iota(jnp.int32, (ROWS, depth), 0)
    column = lax.broadcasted_iota(jnp.int32, (ROWS, depth), 1)
    y_wall = ((row == ROWS - 1) & (tile == 0)) | ((row == rows - 1) & (tile == tiles - 1))
    z_wall = column == depth - 1

    def faces(x, before):
        r = rr_ref[x]
        x_wall = ((x == HALO - 1) & (group == 0)) | ((x == HALO + planes - 1) & (group == groups - 1))
        tx = jnp.where(x_wall, 0.0, 2.0 / (r + rr_ref[x + 1]))
        ty = jnp.where(y_wall, 0.0, 2.0 / (r + pltpu.roll(r, ROWS - 1, 0)))
        tz = jnp.where(z_wall, 0.0, 2.0 / (r + pltpu.roll(r, depth - 1, 1)))
        diagonal = storage + tx + before + ty + pltpu.roll(ty, 1, 0) + tz + pltpu.roll(tz, 1, 1)
        w = RELAX / diagonal
        ws = w * ss_ref[x]
        tx_ref[x] = tx
        ty_ref[x] = ty
        tz_ref[x] = tz
        w_ref[x] = w
        ws_ref[x] = ws
        h_ref[x] = ws
        return tx

    start = 2.0 / (rr_ref[0] + rr_ref[1])
    lax.fori_loop(1, wide - 1, faces, start, unroll=2)

    def second(x, carry):
        total, y_flux, before = carry
        h = h_ref[x]
        tx = tx_ref[x]
        v, ahead = relax(h, h_ref[x + 1], before, tx, ty_ref[x], tz_ref[x], w_ref[x], ws_ref[x], depth)
        v_ref[x] = v
        inside = (x >= HALO) & (x < HALO + planes)
        total = total + jnp.where(inside, ss_ref[x, 0:rows] - storage * v[0:rows], 0.0)
        flux = ty_ref[x] * (v - pltpu.roll(v, ROWS - 1, 0))
        y_flux = y_flux + jnp.where(inside, flux, 0.0)
        return total, y_flux, ahead

    wide_zeros = jnp.zeros((ROWS, depth), jnp.float32)
    first_flow = tx_ref[1] * h_ref[1]
    total, y_flux, _ = lax.fori_loop(
        2, wide - 2, second, (zeros, wide_zeros, first_flow), unroll=2
    )
    left, right = HALO - 1, HALO + planes - 1
    out_left = tx_ref[left, 0:rows] * (v_ref[left + 1, 0:rows] - v_ref[left, 0:rows])
    out_right = tx_ref[right, 0:rows] * (v_ref[right, 0:rows] - v_ref[right + 1, 0:rows])
    side = jnp.where(row == ROWS - 1, y_flux, jnp.where(row == rows - 1, -y_flux, 0.0))
    rhs = total - out_left - out_right + side[0:rows] + side[rows:ROWS]
    rhs = jnp.sum(rhs, keepdims=True)
    link_x = jnp.sum(tx_ref[right, 0:rows], keepdims=True)

    def y_links(x, acc):
        return acc + ty_ref[HALO + x, 0:rows]

    link_y = lax.fori_loop(0, planes, y_links, zeros, unroll=8)
    link_y = jnp.sum(jnp.where(row[0:rows] == rows - 1, link_y, 0.0), keepdims=True)
    lane = lax.broadcasted_iota(jnp.int32, (1, 128), 1) - (32 * group + 4 * y_pos)
    packed = jnp.where(lane == 0, rhs, 0.0) + jnp.where(lane == 1, link_x, 0.0)
    packed = packed + jnp.where(lane == 2, link_y, 0.0)
    for peer in range(sums_ref.shape[0]):
        sums_ref[peer] = packed


def relax(h, h_next, before, tx, ty, tz, w, ws, depth):
    ahead = tx * h
    flow = before + tx * h_next
    flow = flow + ty * pltpu.roll(h, h.shape[0] - 1, 0) + pltpu.roll(ty * h, 1, 0)
    flow = flow + tz * pltpu.roll(h, depth - 1, 1) + pltpu.roll(tz * h, 1, 1)
    return (1.0 - RELAX) * h + ws + w * flow, ahead


def merge_kernel(part_ref, out_ref):
    total = part_ref[0]
    for peer in range(1, part_ref.shape[0]):
        total = total + part_ref[peer]
    for peer in range(out_ref.shape[0]):
        out_ref[peer] = total


def before_by(pair, stride):
    even, odd = pair
    length = even.shape[0]
    if stride == 1:
        return pltpu.roll(odd, 1, 0), even
    shift = stride // 2
    return pltpu.roll(even, shift, 0), pltpu.roll(odd, shift, 0)


def after_by(pair, stride):
    even, odd = pair
    length = even.shape[0]
    if stride == 1:
        return odd, pltpu.roll(even, length - 1, 0)
    shift = length - stride // 2
    return pltpu.roll(even, shift, 0), pltpu.roll(odd, shift, 0)


def each(fn, *pairs):
    return tuple(fn(*values) for values in zip(*pairs, strict=True))


def coarse_solve(sums_ref, store_brick, levels):
    lines = sums_ref.shape[0] // 2
    lanes = sums_ref.shape[2]
    y_lane = lax.broadcasted_iota(jnp.int32, (8, lanes), 1) // 4 % 8
    own_y = y_lane == lax.broadcasted_iota(jnp.int32, (8, lanes), 0)

    def unpack(line):
        line = jnp.where(own_y, jnp.broadcast_to(line, (8, lanes)), 0.0)
        for shift in (16, 8, 4):
            line = line + pltpu.roll(line, lanes - shift, 1)
        return line

    rhs = tuple(
        jnp.concatenate([unpack(sums_ref[2 * z + core]) for z in range(lines)], axis=0)
        for core in range(2)
    )
    link_x = each(lambda a: pltpu.roll(a, lanes - 1, 1), rhs)
    link_y = each(lambda a: pltpu.roll(a, lanes - 2, 1), rhs)
    link_x_before = each(lambda a: pltpu.roll(a, 32, 1), link_x)
    link_y_before = before_by(link_y, 1)
    diagonal = each(lambda a, b, c, d: store_brick + a + b + c + d, link_x, link_x_before, link_y, link_y_before)
    upper = each(lambda a: -a, link_y)
    alphas, gammas = [], []
    for level in range(levels):
        stride = 1 << level
        inverse = each(lambda d: 1.0 / d, diagonal)
        ratio = each(lambda u, i: -u * i, upper, inverse)
        alpha = before_by(ratio, stride)
        gamma = each(lambda u, i: -u * i, upper, after_by(inverse, stride))
        low = before_by(each(lambda q, u: q * u, ratio, upper), stride)
        diagonal = each(lambda d, a, g, u: d + a + g * u, diagonal, low, gamma, upper)
        upper = each(lambda g, u: g * u, gamma, after_by(upper, stride))
        alphas.append(alpha)
        gammas.append(gamma)
    inverse = each(lambda d: 1.0 / d, diagonal)
    correction = None
    for sweep_no in range(COARSE_ITERS):
        now = rhs
        if sweep_no:
            now = each(
                lambda r, a, b, c: r + a * pltpu.roll(c, 32, 1) + b * pltpu.roll(c, lanes - 32, 1),
                rhs, link_x_before, link_x, correction,
            )
        for level in range(levels):
            stride = 1 << level
            now = each(
                lambda n, a, p, g, q: n + a * p + g * q,
                now, alphas[level], before_by(now, stride), gammas[level], after_by(now, stride),
            )
        correction = each(lambda n, i: n * i, now, inverse)
    return correction


def last_kernel(
    store_brick, levels,
    sums_ref, v_ref, tx_ref, ty_ref, tz_ref, w_ref, ws_ref,
    out_ref,
    lines_ref, h_ref, g_ref,
):
    group, tile, core, _ = position()
    planes, rows, depth = out_ref.shape
    even, odd = coarse_solve(sums_ref, store_brick, levels)
    length = even.shape[0]
    for parity, line in ((0, even), (1, odd)):
        lines_ref[parity, 0:8] = jnp.zeros((8, line.shape[1]), jnp.float32)
        lines_ref[parity, 8 : 8 + length] = line
        lines_ref[parity, 8 + length : 16 + length] = jnp.zeros((8, line.shape[1]), jnp.float32)
    half = tile // 2
    here = lines_ref[core, pl.ds(8 + half, 1), :]
    ahead = lines_ref[1 - core, pl.ds(8 + half + core, 1), :]
    behind = lines_ref[1 - core, pl.ds(7 + half + core, 1), :]
    lane = lax.broadcasted_iota(jnp.int32, here.shape, 1)
    row = lax.broadcasted_iota(jnp.int32, (ROWS, depth), 0)

    def shift_of(offset):
        own, up, down = (
            jnp.sum(jnp.where(lane == 32 * (group + offset), line, 0.0), keepdims=True)
            for line in (here, ahead, behind)
        )
        return jnp.where(row < rows, own, jnp.where(row < rows + HALO, up, down))

    shifts = [shift_of(offset) for offset in (-1, 0, 1)]
    for x in (2, 3):
        h_ref[x] = v_ref[x] + shifts[0]
        h_ref[HALO + planes + x - 2] = v_ref[HALO + planes + x - 2] + shifts[2]
    middle = shifts[1]

    def lift(x, carry):
        h_ref[x] = v_ref[x] + middle
        return carry

    lax.fori_loop(HALO, HALO + planes, lift, 0, unroll=4)

    def third(x, before):
        v, ahead = relax(
            h_ref[x], h_ref[x + 1], before, tx_ref[x], ty_ref[x], tz_ref[x], w_ref[x], ws_ref[x], depth
        )
        g_ref[x] = v
        return ahead

    lax.fori_loop(HALO - 1, HALO + planes + 1, third, tx_ref[HALO - 2] * h_ref[HALO - 2], unroll=2)

    def fourth(x, before):
        h = g_ref[x]
        h_own = h[0:rows]
        tx = tx_ref[x, 0:rows]
        tz = tz_ref[x, 0:rows]
        ty = ty_ref[x]
        ahead = tx * h_own
        flow = before + tx * g_ref[x + 1, 0:rows]
        flow = flow + (ty * pltpu.roll(h, ROWS - 1, 0) + pltpu.roll(ty * h, 1, 0))[0:rows]
        flow = flow + tz * pltpu.roll(h_own, depth - 1, 1) + pltpu.roll(tz * h_own, 1, 1)
        out_ref[x - HALO] = (1.0 - RELAX) * h_own + ws_ref[x, 0:rows] + w_ref[x, 0:rows] * flow
        return ahead

    first = tx_ref[HALO - 1, 0:rows] * g_ref[HALO - 1, 0:rows]
    lax.fori_loop(HALO, HALO + planes, fourth, first, unroll=2)


def spread(block, axes):
    return lax.all_to_all(block, axes, 0, 0)


def on_device(facies, perm_table, source):
    planes, rows, depth = source.shape
    storage = 0.01 / rows
    groups = lax.axis_size("group")
    z_size, y_size, cores = (lax.axis_size(a) for a in TILE_AXES)
    tiles = z_size * y_size * cores
    brick = f32(planes, rows, depth)
    r, near, far = call(rows_kernel, (brick, brick, brick), [SMEM, VMEM, VMEM], name="rows")(
        perm_table, facies, source
    )
    pairs = [p for i in range(1, tiles - 1, 2) for p in ((i, i + 1), (i + 1, i))]
    far = lax.ppermute(far, TILE_AXES, pairs)
    near = lax.ppermute(near, "core", [(0, 1), (1, 0)])
    slab = f32(12, rows, depth)
    begin, end = call(planes_kernel, (slab, slab), [VMEM] * 4, name="planes")(r, source, near, far)
    end = lax.ppermute(end, "group", [(i, i + 1) for i in range(groups - 1)])
    begin = lax.ppermute(begin, "group", [(i + 1, i) for i in range(groups - 1)])
    wide = f32(planes + 2 * HALO, ROWS, depth)
    scratch = [pltpu.VMEM(wide.shape, jnp.float32)]
    sums, *fields = call(
        functools.partial(fine_kernel, storage),
        (f32(groups * y_size, 1, 128),) + (wide,) * 6,
        [VMEM] * 6,
        scratch * 3,
        name="fine",
    )(r, source, near, far, begin, end)
    sums = spread(sums, ("group", "y"))
    sums = call(merge_kernel, f32(z_size * cores, 1, 128), [VMEM], name="merge")(sums)
    sums = spread(sums, ("z", "core"))
    length = z_size * y_size
    return call(
        functools.partial(last_kernel, storage * planes * rows * depth, tiles.bit_length() - 1),
        brick,
        [VMEM] * 7,
        [pltpu.VMEM((2, length + 16, 128), jnp.float32)] + scratch * 2,
        name="last",
    )(sums, *fields)


def solution(mesh):
    groups, tiles = mesh.shape["group"], mesh.shape["tile"]
    chips = Mesh(mesh.devices.reshape(groups, tiles // 16, 8, 2), ("group",) + TILE_AXES)
    cells = P("group", TILE_AXES, None)
    return jax.shard_map(
        on_device, mesh=chips, in_specs=(cells, P(), cells), out_specs=cells, check_vma=False
    )
```

```python
import functools

import jax
import jax.numpy as jnp
from jax import lax
from jax.experimental import pallas as pl
from jax.experimental.pallas import tpu as pltpu
from jax.sharding import Mesh
from jax.sharding import PartitionSpec as P

COARSE_ITERS = 3
RELAX = 0.8
HALO = 4
TILE_AXES = ("z", "y", "core")
ROWS = 16
VMEM = pl.BlockSpec(memory_space=pltpu.VMEM)
HBM = pl.BlockSpec(memory_space=pltpu.HBM)


def position():
    z, y, core = (lax.axis_index(a) for a in TILE_AXES)
    tile = (z * lax.axis_size("y") + y) * lax.axis_size("core") + core
    return lax.axis_index("group"), tile, core, y


def call(kernel, out_shape, in_specs, scratch=(), name=None, cost=None):
    outs = jax.tree.map(lambda _: VMEM, out_shape)
    return pl.pallas_call(
        kernel,
        out_shape=out_shape,
        in_specs=in_specs,
        out_specs=outs,
        scratch_shapes=list(scratch),
        name=name,
        cost_estimate=cost,
        compiler_params=pltpu.CompilerParams(vmem_limit_bytes=24 * 1024 * 1024),
    )


def f32(*shape):
    return jax.ShapeDtypeStruct(shape, jnp.float32)


def rows_kernel(
    chunks, table_hbm, facies_hbm, source_hbm, r_ref, source_ref, near_ref, far_ref,
    table_ref, facies_ref, table_sem, sems,
):
    core = position()[2]
    planes, rows, depth = facies_ref.shape
    low = lax.broadcasted_iota(jnp.int32, (rows, depth), 0) < rows // 2
    kinds = table_ref.shape[0]
    first = core == 0
    step = planes // chunks
    table = pltpu.make_async_copy(table_hbm, table_ref, table_sem)
    table.start()
    copies = []
    for chunk in range(chunks):
        part = pl.ds(chunk * step, step)
        pair = (
            pltpu.make_async_copy(facies_hbm.at[part], facies_ref.at[part], sems.at[0, chunk]),
            pltpu.make_async_copy(source_hbm.at[part], source_ref.at[part], sems.at[1, chunk]),
        )
        for copy in pair:
            copy.start()
        copies.append(pair)
    table.wait()

    for chunk in range(chunks):
        for copy in copies[chunk]:
            copy.wait()

        def body(x, carry):
            facies = facies_ref[x]
            perm = jnp.full((rows, depth), table_ref[0], jnp.float32)
            for kind in range(1, kinds):
                perm = jnp.where(facies == kind, table_ref[kind], perm)
            r = 1.0 / perm
            source = source_ref[x]
            r_ref[x] = r
            begin = jnp.where(low, r, pltpu.roll(source, rows // 2, 0))
            end = jnp.where(low, pltpu.roll(r, rows // 2, 0), source)
            near_ref[x] = jnp.where(first, end, begin)
            far_ref[x] = jnp.where(first, begin, end)
            return carry

        lax.fori_loop(chunk * step, (chunk + 1) * step, body, 0, unroll=8)


def halo_rows(near_ref, far_ref, x, core, tile, tiles):
    rows = far_ref.shape[1]
    depth = far_ref.shape[2]
    low = lax.broadcasted_iota(jnp.int32, (rows, depth), 0) < rows // 2
    near = near_ref[x]
    far = far_ref[x]
    first = core == 0
    after = jnp.where(first, near, far)
    before = jnp.where(first, far, near)
    r = jnp.where(low, after, pltpu.roll(before, rows // 2, 0))
    source = jnp.where(low, pltpu.roll(after, rows // 2, 0), before)
    absent = (low & (tile == tiles - 1)) | (~low & (tile == 0))
    return jnp.where(absent, 1.0, r), jnp.where(absent, 0.0, source)


def planes_kernel(r_ref, source_ref, near_ref, far_ref, begin_ref, end_ref):
    _, tile, core, _ = position()
    tiles = lax.axis_size("z") * lax.axis_size("y") * lax.axis_size("core")
    planes = r_ref.shape[0]
    for d in range(HALO):
        for out, x in ((begin_ref, d), (end_ref, planes - 1 - d)):
            out[d] = r_ref[x]
            if d < HALO - 1:
                side_r, side_source = halo_rows(near_ref, far_ref, x, core, tile, tiles)
                out[4 + d] = side_r
                out[7 + d] = source_ref[x]
                if d < HALO - 2:
                    out[10 + d] = side_source


def fine_kernel(
    storage,
    r_ref, source_ref, near_ref, far_ref, begin_ref, end_ref,
    sums_ref, v_ref, tx_ref, ty_ref, tz_ref, w_ref, ws_ref,
    rr_ref, ss_ref, h_ref,
):
    group, tile, core, y_pos = position()
    groups = lax.axis_size("group")
    tiles = lax.axis_size("z") * lax.axis_size("y") * lax.axis_size("core")
    planes, rows, depth = r_ref.shape
    wide = planes + 2 * HALO
    ones = jnp.ones((rows, depth), jnp.float32)
    zeros = jnp.zeros((rows, depth), jnp.float32)
    for d in range(HALO):
        for recv, x, there in (
            (end_ref, HALO - 1 - d, group > 0),
            (begin_ref, HALO + planes + d, group < groups - 1),
        ):
            rr_ref[x, 0:rows] = jnp.where(there, recv[d], 1.0)
            rr_ref[x, rows:ROWS] = jnp.where(there, recv[4 + d], 1.0) if d < HALO - 1 else ones
            ss_ref[x, 0:rows] = jnp.where(there, recv[7 + d], 0.0) if d < HALO - 1 else zeros
            ss_ref[x, rows:ROWS] = jnp.where(there, recv[10 + d], 0.0) if d < HALO - 2 else zeros

    def gather_rows(x, carry):
        side_r, side_source = halo_rows(near_ref, far_ref, x, core, tile, tiles)
        rr_ref[HALO + x, 0:rows] = r_ref[x]
        rr_ref[HALO + x, rows:ROWS] = side_r
        ss_ref[HALO + x, 0:rows] = source_ref[x]
        ss_ref[HALO + x, rows:ROWS] = side_source
        return carry

    lax.fori_loop(0, planes, gather_rows, 0, unroll=16)

    row = lax.broadcasted_iota(jnp.int32, (ROWS, depth), 0)
    column = lax.broadcasted_iota(jnp.int32, (ROWS, depth), 1)
    y_wall = ((row == ROWS - 1) & (tile == 0)) | ((row == rows - 1) & (tile == tiles - 1))
    z_wall = column == depth - 1

    def faces(x, before):
        r = rr_ref[x]
        x_wall = ((x == HALO - 1) & (group == 0)) | ((x == HALO + planes - 1) & (group == groups - 1))
        tx = jnp.where(x_wall, 0.0, 2.0 / (r + rr_ref[x + 1]))
        ty = jnp.where(y_wall, 0.0, 2.0 / (r + pltpu.roll(r, ROWS - 1, 0)))
        tz = jnp.where(z_wall, 0.0, 2.0 / (r + pltpu.roll(r, depth - 1, 1)))
        diagonal = storage + tx + before + ty + pltpu.roll(ty, 1, 0) + tz + pltpu.roll(tz, 1, 1)
        w = RELAX / diagonal
        ws = w * ss_ref[x]
        tx_ref[x] = tx
        ty_ref[x] = ty
        tz_ref[x] = tz
        w_ref[x] = w
        ws_ref[x] = ws
        h_ref[x] = ws
        return tx

    start = 2.0 / (rr_ref[0] + rr_ref[1])
    lax.fori_loop(1, wide - 1, faces, start, unroll=16)

    def second(x, carry):
        total, y_flux, before = carry
        h = h_ref[x]
        tx = tx_ref[x]
        v, ahead = relax(h, h_ref[x + 1], before, tx, ty_ref[x], tz_ref[x], w_ref[x], ws_ref[x], depth)
        v_ref[x] = v
        inside = (x >= HALO) & (x < HALO + planes)
        total = total + jnp.where(inside, ss_ref[x, 0:rows] - storage * v[0:rows], 0.0)
        flux = ty_ref[x] * (v - pltpu.roll(v, ROWS - 1, 0))
        y_flux = y_flux + jnp.where(inside, flux, 0.0)
        return total, y_flux, ahead

    wide_zeros = jnp.zeros((ROWS, depth), jnp.float32)
    first_flow = tx_ref[1] * h_ref[1]
    total, y_flux, _ = lax.fori_loop(
        2, wide - 2, second, (zeros, wide_zeros, first_flow), unroll=16
    )
    left, right = HALO - 1, HALO + planes - 1
    out_left = tx_ref[left, 0:rows] * (v_ref[left + 1, 0:rows] - v_ref[left, 0:rows])
    out_right = tx_ref[right, 0:rows] * (v_ref[right, 0:rows] - v_ref[right + 1, 0:rows])
    side = jnp.where(row == ROWS - 1, y_flux, jnp.where(row == rows - 1, -y_flux, 0.0))
    rhs = total - out_left - out_right + side[0:rows] + side[rows:ROWS]
    rhs = jnp.sum(rhs, keepdims=True)
    link_x = jnp.sum(tx_ref[right, 0:rows], keepdims=True)

    def y_links(x, acc):
        return acc + ty_ref[HALO + x, 0:rows]

    link_y = lax.fori_loop(0, planes, y_links, zeros, unroll=8)
    link_y = jnp.sum(jnp.where(row[0:rows] == rows - 1, link_y, 0.0), keepdims=True)
    lane = lax.broadcasted_iota(jnp.int32, (1, 128), 1) - (32 * group + 4 * y_pos)
    packed = jnp.where(lane == 0, rhs, 0.0) + jnp.where(lane == 1, link_x, 0.0)
    packed = packed + jnp.where(lane == 2, link_y, 0.0)
    for peer in range(sums_ref.shape[0]):
        sums_ref[peer] = packed


def relax(h, h_next, before, tx, ty, tz, w, ws, depth):
    ahead = tx * h
    flow = before + tx * h_next
    flow = flow + ty * pltpu.roll(h, h.shape[0] - 1, 0) + pltpu.roll(ty * h, 1, 0)
    flow = flow + tz * pltpu.roll(h, depth - 1, 1) + pltpu.roll(tz * h, 1, 1)
    return (1.0 - RELAX) * h + ws + w * flow, ahead


def merge_kernel(part_ref, out_ref):
    total = part_ref[0]
    for peer in range(1, part_ref.shape[0]):
        total = total + part_ref[peer]
    for peer in range(out_ref.shape[0]):
        out_ref[peer] = total


def before_by(pair, stride):
    even, odd = pair
    length = even.shape[0]
    if stride == 1:
        return pltpu.roll(odd, 1, 0), even
    shift = stride // 2
    return pltpu.roll(even, shift, 0), pltpu.roll(odd, shift, 0)


def after_by(pair, stride):
    even, odd = pair
    length = even.shape[0]
    if stride == 1:
        return odd, pltpu.roll(even, length - 1, 0)
    shift = length - stride // 2
    return pltpu.roll(even, shift, 0), pltpu.roll(odd, shift, 0)


def each(fn, *pairs):
    return tuple(fn(*values) for values in zip(*pairs, strict=True))


def coarse_solve(sums_ref, store_brick, levels):
    lines = sums_ref.shape[0] // 2
    lanes = sums_ref.shape[2]
    y_lane = lax.broadcasted_iota(jnp.int32, (8, lanes), 1) // 4 % 8
    own_y = y_lane == lax.broadcasted_iota(jnp.int32, (8, lanes), 0)

    def unpack(line):
        line = jnp.where(own_y, jnp.broadcast_to(line, (8, lanes)), 0.0)
        for shift in (16, 8, 4):
            line = line + pltpu.roll(line, lanes - shift, 1)
        return line

    rhs = tuple(
        jnp.concatenate([unpack(sums_ref[2 * z + core]) for z in range(lines)], axis=0)
        for core in range(2)
    )
    link_x = each(lambda a: pltpu.roll(a, lanes - 1, 1), rhs)
    link_y = each(lambda a: pltpu.roll(a, lanes - 2, 1), rhs)
    link_x_before = each(lambda a: pltpu.roll(a, 32, 1), link_x)
    link_y_before = before_by(link_y, 1)
    diagonal = each(lambda a, b, c, d: store_brick + a + b + c + d, link_x, link_x_before, link_y, link_y_before)
    upper = each(lambda a: -a, link_y)
    alphas, gammas = [], []
    for level in range(levels):
        stride = 1 << level
        inverse = each(lambda d: 1.0 / d, diagonal)
        ratio = each(lambda u, i: -u * i, upper, inverse)
        alpha = before_by(ratio, stride)
        gamma = each(lambda u, i: -u * i, upper, after_by(inverse, stride))
        low = before_by(each(lambda q, u: q * u, ratio, upper), stride)
        diagonal = each(lambda d, a, g, u: d + a + g * u, diagonal, low, gamma, upper)
        upper = each(lambda g, u: g * u, gamma, after_by(upper, stride))
        alphas.append(alpha)
        gammas.append(gamma)
    inverse = each(lambda d: 1.0 / d, diagonal)
    correction = None
    for sweep_no in range(COARSE_ITERS):
        now = rhs
        if sweep_no:
            now = each(
                lambda r, a, b, c: r + a * pltpu.roll(c, 32, 1) + b * pltpu.roll(c, lanes - 32, 1),
                rhs, link_x_before, link_x, correction,
            )
        for level in range(levels):
            stride = 1 << level
            now = each(
                lambda n, a, p, g, q: n + a * p + g * q,
                now, alphas[level], before_by(now, stride), gammas[level], after_by(now, stride),
            )
        correction = each(lambda n, i: n * i, now, inverse)
    return correction


def last_kernel(
    store_brick, levels,
    sums_ref, v_ref, tx_ref, ty_ref, tz_ref, w_ref, ws_ref,
    out_ref,
    lines_ref, h_ref, g_ref,
):
    group, tile, core, _ = position()
    planes, rows, depth = out_ref.shape
    even, odd = coarse_solve(sums_ref, store_brick, levels)
    length = even.shape[0]
    for parity, line in ((0, even), (1, odd)):
        lines_ref[parity, 0:8] = jnp.zeros((8, line.shape[1]), jnp.float32)
        lines_ref[parity, 8 : 8 + length] = line
        lines_ref[parity, 8 + length : 16 + length] = jnp.zeros((8, line.shape[1]), jnp.float32)
    half = tile // 2
    here = lines_ref[core, pl.ds(8 + half, 1), :]
    ahead = lines_ref[1 - core, pl.ds(8 + half + core, 1), :]
    behind = lines_ref[1 - core, pl.ds(7 + half + core, 1), :]
    lane = lax.broadcasted_iota(jnp.int32, here.shape, 1)
    row = lax.broadcasted_iota(jnp.int32, (ROWS, depth), 0)

    def shift_of(offset):
        own, up, down = (
            jnp.sum(jnp.where(lane == 32 * (group + offset), line, 0.0), keepdims=True)
            for line in (here, ahead, behind)
        )
        return jnp.where(row < rows, own, jnp.where(row < rows + HALO, up, down))

    shifts = [shift_of(offset) for offset in (-1, 0, 1)]
    for x in (2, 3):
        h_ref[x] = v_ref[x] + shifts[0]
        h_ref[HALO + planes + x - 2] = v_ref[HALO + planes + x - 2] + shifts[2]
    middle = shifts[1]

    def lift(x, carry):
        h_ref[x] = v_ref[x] + middle
        return carry

    lax.fori_loop(HALO, HALO + planes, lift, 0, unroll=4)

    def third(x, before):
        v, ahead = relax(
            h_ref[x], h_ref[x + 1], before, tx_ref[x], ty_ref[x], tz_ref[x], w_ref[x], ws_ref[x], depth
        )
        g_ref[x] = v
        return ahead

    lax.fori_loop(HALO - 1, HALO + planes + 1, third, tx_ref[HALO - 2] * h_ref[HALO - 2], unroll=16)

    def fourth(x, before):
        h = g_ref[x]
        h_own = h[0:rows]
        tx = tx_ref[x, 0:rows]
        tz = tz_ref[x, 0:rows]
        ty = ty_ref[x]
        ahead = tx * h_own
        flow = before + tx * g_ref[x + 1, 0:rows]
        flow = flow + (ty * pltpu.roll(h, ROWS - 1, 0) + pltpu.roll(ty * h, 1, 0))[0:rows]
        flow = flow + tz * pltpu.roll(h_own, depth - 1, 1) + pltpu.roll(tz * h_own, 1, 1)
        out_ref[x - HALO] = (1.0 - RELAX) * h_own + ws_ref[x, 0:rows] + w_ref[x, 0:rows] * flow
        return ahead

    first = tx_ref[HALO - 1, 0:rows] * g_ref[HALO - 1, 0:rows]
    lax.fori_loop(HALO, HALO + planes, fourth, first, unroll=16)


def spread(block, axes):
    return lax.all_to_all(block, axes, 0, 0)


def on_device(facies, perm_table, source):
    planes, rows, depth = source.shape
    storage = 0.01 / rows
    groups = lax.axis_size("group")
    z_size, y_size, cores = (lax.axis_size(a) for a in TILE_AXES)
    tiles = z_size * y_size * cores
    brick = f32(planes, rows, depth)
    chunks = 4
    r, source, near, far = call(
        functools.partial(rows_kernel, chunks),
        (brick,) * 4,
        [HBM] * 3,
        [
            pltpu.SMEM(perm_table.shape, jnp.float32),
            pltpu.VMEM(source.shape, jnp.int32),
            pltpu.SemaphoreType.DMA,
            pltpu.SemaphoreType.DMA((2, chunks)),
        ],
        name="rows",
    )(*(pltpu.with_memory_space_constraint(a, pltpu.HBM) for a in (perm_table, facies, source)))
    pairs = [p for i in range(1, tiles - 1, 2) for p in ((i, i + 1), (i + 1, i))]
    far = lax.ppermute(far, TILE_AXES, pairs)
    near = lax.ppermute(near, "core", [(0, 1), (1, 0)])
    slab = f32(12, rows, depth)
    begin, end = call(planes_kernel, (slab, slab), [VMEM] * 4, name="planes")(r, source, near, far)
    end = lax.ppermute(end, "group", [(i, i + 1) for i in range(groups - 1)])
    begin = lax.ppermute(begin, "group", [(i + 1, i) for i in range(groups - 1)])
    wide = f32(planes + 2 * HALO, ROWS, depth)
    scratch = [pltpu.VMEM(wide.shape, jnp.float32)]
    sums, *fields = call(
        functools.partial(fine_kernel, storage),
        (f32(groups * y_size, 1, 128),) + (wide,) * 6,
        [VMEM] * 6,
        scratch * 3,
        name="fine",
    )(r, source, near, far, begin, end)
    sums = spread(sums, ("group", "y"))
    sums = call(merge_kernel, f32(z_size * cores, 1, 128), [VMEM], name="merge")(sums)
    sums = spread(sums, ("z", "core"))
    length = z_size * y_size
    return call(
        functools.partial(last_kernel, storage * planes * rows * depth, tiles.bit_length() - 1),
        brick,
        [VMEM] * 7,
        [pltpu.VMEM((2, length + 16, 128), jnp.float32)] + scratch * 2,
        name="last",
    )(sums, *fields)


def solution(mesh):
    groups, tiles = mesh.shape["group"], mesh.shape["tile"]
    chips = Mesh(mesh.devices.reshape(groups, tiles // 16, 8, 2), ("group",) + TILE_AXES)
    cells = P("group", TILE_AXES, None)
    return jax.shard_map(
        on_device, mesh=chips, in_specs=(cells, P(), cells), out_specs=cells, check_vma=False
    )
```

```python
import functools

import jax
import jax.numpy as jnp
from jax import lax
from jax.experimental import pallas as pl
from jax.experimental.pallas import tpu as pltpu
from jax.sharding import Mesh
from jax.sharding import PartitionSpec as P

COARSE_ITERS = 3
RELAX = 0.8
HALO = 4
TILE_AXES = ("z", "y", "core")
ROWS = 16
VMEM = pl.BlockSpec(memory_space=pltpu.VMEM)
HBM = pl.BlockSpec(memory_space=pltpu.HBM)


def position():
    z, y, core = (lax.axis_index(a) for a in TILE_AXES)
    tile = (z * lax.axis_size("y") + y) * lax.axis_size("core") + core
    return lax.axis_index("group"), tile, core, y


def call(kernel, out_shape, in_specs, scratch=(), name=None, cost=None):
    outs = jax.tree.map(lambda _: VMEM, out_shape)
    return pl.pallas_call(
        kernel,
        out_shape=out_shape,
        in_specs=in_specs,
        out_specs=outs,
        scratch_shapes=list(scratch),
        name=name,
        cost_estimate=cost,
        compiler_params=pltpu.CompilerParams(vmem_limit_bytes=24 * 1024 * 1024),
    )


def f32(*shape):
    return jax.ShapeDtypeStruct(shape, jnp.float32)


def low_half(shape):
    return lax.broadcasted_iota(jnp.int32, shape, 0) < shape[0] // 2


def row_tiles(r, source):
    low = low_half(r.shape)
    half = r.shape[0] // 2
    return jnp.where(low, r, pltpu.roll(source, half, 0)), jnp.where(low, pltpu.roll(r, half, 0), source)


def rows_kernel(
    chunks, table_hbm, facies_hbm, source_hbm, r_ref, source_ref, near_ref, far_ref,
    table_ref, facies_ref, table_sem, sems,
):
    core = position()[2]
    planes, rows, depth = facies_ref.shape
    kinds = table_ref.shape[0]
    first = core == 0
    step = planes // chunks
    table = pltpu.make_async_copy(table_hbm, table_ref, table_sem)
    table.start()
    copies = []
    for chunk in range(chunks):
        part = pl.ds(chunk * step, step)
        pair = (
            pltpu.make_async_copy(facies_hbm.at[part], facies_ref.at[part], sems.at[0, chunk]),
            pltpu.make_async_copy(source_hbm.at[part], source_ref.at[part], sems.at[1, chunk]),
        )
        for copy in pair:
            copy.start()
        copies.append(pair)
    table.wait()

    for chunk in range(chunks):
        for copy in copies[chunk]:
            copy.wait()

        def body(x, carry):
            facies = facies_ref[x]
            perm = jnp.full((rows, depth), table_ref[0], jnp.float32)
            for kind in range(1, kinds):
                perm = jnp.where(facies == kind, table_ref[kind], perm)
            r = 1.0 / perm
            source = source_ref[x]
            r_ref[x] = r
            begin, end = row_tiles(r, source)
            near_ref[x] = jnp.where(first, end, begin)
            far_ref[x] = jnp.where(first, begin, end)
            return carry

        lax.fori_loop(chunk * step, (chunk + 1) * step, body, 0, unroll=8)


def halo_rows(near, far, core, tile, tiles):
    low = low_half(near.shape)
    first = core == 0
    after = jnp.where(first, near, far)
    before = jnp.where(first, far, near)
    half = near.shape[0] // 2
    r = jnp.where(low, after, pltpu.roll(before, half, 0))
    source = jnp.where(low, pltpu.roll(after, half, 0), before)
    absent = (low & (tile == tiles - 1)) | (~low & (tile == 0))
    return jnp.where(absent, 1.0, r), jnp.where(absent, 0.0, source)


def planes_kernel(r_ref, source_ref, near_ref, begin_ref, end_ref):
    planes = r_ref.shape[0]
    for d in range(HALO):
        for out, x in ((begin_ref, d), (end_ref, planes - 1 - d)):
            out[d] = r_ref[x]
            if d < HALO - 1:
                out[4 + d] = near_ref[x]
                out[7 + d] = source_ref[x]


def corners_kernel(begin_ref, end_ref, out_ref):
    first = position()[2] == 0
    for side, recv in enumerate((begin_ref, end_ref)):
        for d in range(HALO - 1):
            begin, end = row_tiles(recv[d], recv[7 + d])
            out_ref[3 * side + d] = jnp.where(first, begin, end)


def fine_kernel(
    storage,
    r_ref, source_ref, near_ref, far_ref, begin_ref, end_ref, corner_ref,
    sums_ref, v_ref, tx_ref, ty_ref, tz_ref, w_ref, ws_ref,
    rr_ref, ss_ref, h_ref,
):
    group, tile, core, y_pos = position()
    groups = lax.axis_size("group")
    tiles = lax.axis_size("z") * lax.axis_size("y") * lax.axis_size("core")
    planes, rows, depth = r_ref.shape
    wide = planes + 2 * HALO
    ones = jnp.ones((rows, depth), jnp.float32)
    zeros = jnp.zeros((rows, depth), jnp.float32)
    for d in range(HALO):
        for side, recv, x, there in (
            (1, end_ref, HALO - 1 - d, group > 0),
            (0, begin_ref, HALO + planes + d, group < groups - 1),
        ):
            side_r, side_source, own_source = ones, zeros, zeros
            if d < HALO - 1:
                far = corner_ref[3 * side + d]
                side_r, side_source = halo_rows(recv[4 + d], far, core, tile, tiles)
                own_source = recv[7 + d]
            rr_ref[x, 0:rows] = jnp.where(there, recv[d], 1.0)
            rr_ref[x, rows:ROWS] = jnp.where(there, side_r, 1.0)
            ss_ref[x, 0:rows] = jnp.where(there, own_source, 0.0)
            ss_ref[x, rows:ROWS] = jnp.where(there, side_source, 0.0)

    def gather_rows(x, carry):
        side_r, side_source = halo_rows(near_ref[x], far_ref[x], core, tile, tiles)
        rr_ref[HALO + x, 0:rows] = r_ref[x]
        rr_ref[HALO + x, rows:ROWS] = side_r
        ss_ref[HALO + x, 0:rows] = source_ref[x]
        ss_ref[HALO + x, rows:ROWS] = side_source
        return carry

    lax.fori_loop(0, planes, gather_rows, 0, unroll=16)

    row = lax.broadcasted_iota(jnp.int32, (ROWS, depth), 0)
    column = lax.broadcasted_iota(jnp.int32, (ROWS, depth), 1)
    y_wall = ((row == ROWS - 1) & (tile == 0)) | ((row == rows - 1) & (tile == tiles - 1))
    z_wall = column == depth - 1

    def faces(x, before):
        r = rr_ref[x]
        x_wall = ((x == HALO - 1) & (group == 0)) | ((x == HALO + planes - 1) & (group == groups - 1))
        tx = jnp.where(x_wall, 0.0, 2.0 / (r + rr_ref[x + 1]))
        ty = jnp.where(y_wall, 0.0, 2.0 / (r + pltpu.roll(r, ROWS - 1, 0)))
        tz = jnp.where(z_wall, 0.0, 2.0 / (r + pltpu.roll(r, depth - 1, 1)))
        diagonal = storage + tx + before + ty + pltpu.roll(ty, 1, 0) + tz + pltpu.roll(tz, 1, 1)
        w = RELAX / diagonal
        ws = w * ss_ref[x]
        tx_ref[x] = tx
        ty_ref[x] = ty
        tz_ref[x] = tz
        w_ref[x] = w
        ws_ref[x] = ws
        h_ref[x] = ws
        return tx

    start = 2.0 / (rr_ref[0] + rr_ref[1])
    lax.fori_loop(1, wide - 1, faces, start, unroll=16)

    def second(x, carry):
        total, y_flux, before = carry
        h = h_ref[x]
        tx = tx_ref[x]
        v, ahead = relax(h, h_ref[x + 1], before, tx, ty_ref[x], tz_ref[x], w_ref[x], ws_ref[x], depth)
        v_ref[x] = v
        inside = (x >= HALO) & (x < HALO + planes)
        total = total + jnp.where(inside, ss_ref[x, 0:rows] - storage * v[0:rows], 0.0)
        flux = ty_ref[x] * (v - pltpu.roll(v, ROWS - 1, 0))
        y_flux = y_flux + jnp.where(inside, flux, 0.0)
        return total, y_flux, ahead

    wide_zeros = jnp.zeros((ROWS, depth), jnp.float32)
    first_flow = tx_ref[1] * h_ref[1]
    total, y_flux, _ = lax.fori_loop(
        2, wide - 2, second, (zeros, wide_zeros, first_flow), unroll=16
    )
    left, right = HALO - 1, HALO + planes - 1
    out_left = tx_ref[left, 0:rows] * (v_ref[left + 1, 0:rows] - v_ref[left, 0:rows])
    out_right = tx_ref[right, 0:rows] * (v_ref[right, 0:rows] - v_ref[right + 1, 0:rows])
    side = jnp.where(row == ROWS - 1, y_flux, jnp.where(row == rows - 1, -y_flux, 0.0))
    rhs = total - out_left - out_right + side[0:rows] + side[rows:ROWS]
    rhs = jnp.sum(rhs, keepdims=True)
    link_x = jnp.sum(tx_ref[right, 0:rows], keepdims=True)

    def y_links(x, acc):
        return acc + ty_ref[HALO + x, 0:rows]

    link_y = lax.fori_loop(0, planes, y_links, zeros, unroll=8)
    link_y = jnp.sum(jnp.where(row[0:rows] == rows - 1, link_y, 0.0), keepdims=True)
    lane = lax.broadcasted_iota(jnp.int32, (1, 128), 1) - (32 * group + 4 * y_pos)
    packed = jnp.where(lane == 0, rhs, 0.0) + jnp.where(lane == 1, link_x, 0.0)
    packed = packed + jnp.where(lane == 2, link_y, 0.0)
    for peer in range(sums_ref.shape[0]):
        sums_ref[peer] = packed


def relax(h, h_next, before, tx, ty, tz, w, ws, depth):
    ahead = tx * h
    flow = before + tx * h_next
    flow = flow + ty * pltpu.roll(h, h.shape[0] - 1, 0) + pltpu.roll(ty * h, 1, 0)
    flow = flow + tz * pltpu.roll(h, depth - 1, 1) + pltpu.roll(tz * h, 1, 1)
    return (1.0 - RELAX) * h + ws + w * flow, ahead


def merge_kernel(part_ref, out_ref):
    total = part_ref[0]
    for peer in range(1, part_ref.shape[0]):
        total = total + part_ref[peer]
    for peer in range(out_ref.shape[0]):
        out_ref[peer] = total


def before_by(pair, stride):
    even, odd = pair
    length = even.shape[0]
    if stride == 1:
        return pltpu.roll(odd, 1, 0), even
    shift = stride // 2
    return pltpu.roll(even, shift, 0), pltpu.roll(odd, shift, 0)


def after_by(pair, stride):
    even, odd = pair
    length = even.shape[0]
    if stride == 1:
        return odd, pltpu.roll(even, length - 1, 0)
    shift = length - stride // 2
    return pltpu.roll(even, shift, 0), pltpu.roll(odd, shift, 0)


def each(fn, *pairs):
    return tuple(fn(*values) for values in zip(*pairs, strict=True))


def coarse_solve(sums_ref, store_brick, levels):
    lines = sums_ref.shape[0] // 2
    lanes = sums_ref.shape[2]
    y_lane = lax.broadcasted_iota(jnp.int32, (8, lanes), 1) // 4 % 8
    own_y = y_lane == lax.broadcasted_iota(jnp.int32, (8, lanes), 0)

    def unpack(line):
        line = jnp.where(own_y, jnp.broadcast_to(line, (8, lanes)), 0.0)
        for shift in (16, 8, 4):
            line = line + pltpu.roll(line, lanes - shift, 1)
        return line

    rhs = tuple(
        jnp.concatenate([unpack(sums_ref[2 * z + core]) for z in range(lines)], axis=0)
        for core in range(2)
    )
    link_x = each(lambda a: pltpu.roll(a, lanes - 1, 1), rhs)
    link_y = each(lambda a: pltpu.roll(a, lanes - 2, 1), rhs)
    link_x_before = each(lambda a: pltpu.roll(a, 32, 1), link_x)
    link_y_before = before_by(link_y, 1)
    diagonal = each(lambda a, b, c, d: store_brick + a + b + c + d, link_x, link_x_before, link_y, link_y_before)
    upper = each(lambda a: -a, link_y)
    alphas, gammas = [], []
    for level in range(levels):
        stride = 1 << level
        inverse = each(lambda d: 1.0 / d, diagonal)
        ratio = each(lambda u, i: -u * i, upper, inverse)
        alpha = before_by(ratio, stride)
        gamma = each(lambda u, i: -u * i, upper, after_by(inverse, stride))
        low = before_by(each(lambda q, u: q * u, ratio, upper), stride)
        diagonal = each(lambda d, a, g, u: d + a + g * u, diagonal, low, gamma, upper)
        upper = each(lambda g, u: g * u, gamma, after_by(upper, stride))
        alphas.append(alpha)
        gammas.append(gamma)
    inverse = each(lambda d: 1.0 / d, diagonal)
    correction = None
    for sweep_no in range(COARSE_ITERS):
        now = rhs
        if sweep_no:
            now = each(
                lambda r, a, b, c: r + a * pltpu.roll(c, 32, 1) + b * pltpu.roll(c, lanes - 32, 1),
                rhs, link_x_before, link_x, correction,
            )
        for level in range(levels):
            stride = 1 << level
            now = each(
                lambda n, a, p, g, q: n + a * p + g * q,
                now, alphas[level], before_by(now, stride), gammas[level], after_by(now, stride),
            )
        correction = each(lambda n, i: n * i, now, inverse)
    return correction


def last_kernel(
    store_brick, levels,
    sums_ref, v_ref, tx_ref, ty_ref, tz_ref, w_ref, ws_ref,
    out_ref,
    lines_ref, h_ref, g_ref,
):
    group, tile, core, _ = position()
    planes, rows, depth = out_ref.shape
    even, odd = coarse_solve(sums_ref, store_brick, levels)
    length = even.shape[0]
    for parity, line in ((0, even), (1, odd)):
        lines_ref[parity, 0:8] = jnp.zeros((8, line.shape[1]), jnp.float32)
        lines_ref[parity, 8 : 8 + length] = line
        lines_ref[parity, 8 + length : 16 + length] = jnp.zeros((8, line.shape[1]), jnp.float32)
    half = tile // 2
    here = lines_ref[core, pl.ds(8 + half, 1), :]
    ahead = lines_ref[1 - core, pl.ds(8 + half + core, 1), :]
    behind = lines_ref[1 - core, pl.ds(7 + half + core, 1), :]
    lane = lax.broadcasted_iota(jnp.int32, here.shape, 1)
    row = lax.broadcasted_iota(jnp.int32, (ROWS, depth), 0)

    def shift_of(offset):
        own, up, down = (
            jnp.sum(jnp.where(lane == 32 * (group + offset), line, 0.0), keepdims=True)
            for line in (here, ahead, behind)
        )
        return jnp.where(row < rows, own, jnp.where(row < rows + HALO, up, down))

    shifts = [shift_of(offset) for offset in (-1, 0, 1)]
    for x in (2, 3):
        h_ref[x] = v_ref[x] + shifts[0]
        h_ref[HALO + planes + x - 2] = v_ref[HALO + planes + x - 2] + shifts[2]
    middle = shifts[1]

    def lift(x, carry):
        h_ref[x] = v_ref[x] + middle
        return carry

    lax.fori_loop(HALO, HALO + planes, lift, 0, unroll=4)

    def third(x, before):
        v, ahead = relax(
            h_ref[x], h_ref[x + 1], before, tx_ref[x], ty_ref[x], tz_ref[x], w_ref[x], ws_ref[x], depth
        )
        g_ref[x] = v
        return ahead

    lax.fori_loop(HALO - 1, HALO + planes + 1, third, tx_ref[HALO - 2] * h_ref[HALO - 2], unroll=16)

    def fourth(x, before):
        h = g_ref[x]
        h_own = h[0:rows]
        tx = tx_ref[x, 0:rows]
        tz = tz_ref[x, 0:rows]
        ty = ty_ref[x]
        ahead = tx * h_own
        flow = before + tx * g_ref[x + 1, 0:rows]
        flow = flow + (ty * pltpu.roll(h, ROWS - 1, 0) + pltpu.roll(ty * h, 1, 0))[0:rows]
        flow = flow + tz * pltpu.roll(h_own, depth - 1, 1) + pltpu.roll(tz * h_own, 1, 1)
        out_ref[x - HALO] = (1.0 - RELAX) * h_own + ws_ref[x, 0:rows] + w_ref[x, 0:rows] * flow
        return ahead

    first = tx_ref[HALO - 1, 0:rows] * g_ref[HALO - 1, 0:rows]
    lax.fori_loop(HALO, HALO + planes, fourth, first, unroll=16)


def spread(block, axes):
    return lax.all_to_all(block, axes, 0, 0)


def on_device(facies, perm_table, source):
    planes, rows, depth = source.shape
    storage = 0.01 / rows
    groups = lax.axis_size("group")
    z_size, y_size, cores = (lax.axis_size(a) for a in TILE_AXES)
    tiles = z_size * y_size * cores
    brick = f32(planes, rows, depth)
    chunks = 4
    r, source, near, far = call(
        functools.partial(rows_kernel, chunks),
        (brick,) * 4,
        [HBM] * 3,
        [
            pltpu.SMEM(perm_table.shape, jnp.float32),
            pltpu.VMEM(source.shape, jnp.int32),
            pltpu.SemaphoreType.DMA,
            pltpu.SemaphoreType.DMA((2, chunks)),
        ],
        name="rows",
    )(*(pltpu.with_memory_space_constraint(a, pltpu.HBM) for a in (perm_table, facies, source)))
    pairs = [p for i in range(1, tiles - 1, 2) for p in ((i, i + 1), (i + 1, i))]
    far = lax.ppermute(far, TILE_AXES, pairs)
    near = lax.ppermute(near, "core", [(0, 1), (1, 0)])
    slab = f32(10, rows, depth)
    begin, end = call(planes_kernel, (slab, slab), [VMEM] * 3, name="planes")(r, source, near)
    end = lax.ppermute(end, "group", [(i, i + 1) for i in range(groups - 1)])
    begin = lax.ppermute(begin, "group", [(i + 1, i) for i in range(groups - 1)])
    corner = call(corners_kernel, f32(6, rows, depth), [VMEM] * 2, name="corners")(begin, end)
    corner = lax.ppermute(corner, TILE_AXES, pairs)
    wide = f32(planes + 2 * HALO, ROWS, depth)
    scratch = [pltpu.VMEM(wide.shape, jnp.float32)]
    sums, *fields = call(
        functools.partial(fine_kernel, storage),
        (f32(groups * y_size, 1, 128),) + (wide,) * 6,
        [VMEM] * 7,
        scratch * 3,
        name="fine",
    )(r, source, near, far, begin, end, corner)
    sums = spread(sums, ("group", "y"))
    sums = call(merge_kernel, f32(z_size * cores, 1, 128), [VMEM], name="merge")(sums)
    sums = spread(sums, ("z", "core"))
    length = z_size * y_size
    return call(
        functools.partial(last_kernel, storage * planes * rows * depth, tiles.bit_length() - 1),
        brick,
        [VMEM] * 7,
        [pltpu.VMEM((2, length + 16, 128), jnp.float32)] + scratch * 2,
        name="last",
    )(sums, *fields)


def solution(mesh):
    groups, tiles = mesh.shape["group"], mesh.shape["tile"]
    chips = Mesh(mesh.devices.reshape(groups, tiles // 16, 8, 2), ("group",) + TILE_AXES)
    cells = P("group", TILE_AXES, None)
    return jax.shard_map(
        on_device, mesh=chips, in_specs=(cells, P(), cells), out_specs=cells, check_vma=False
    )
```

```python
import functools

import jax
import jax.numpy as jnp
from jax import lax
from jax.experimental import pallas as pl
from jax.experimental.pallas import tpu as pltpu
from jax.sharding import Mesh
from jax.sharding import PartitionSpec as P

COARSE_ITERS = 3
RELAX = 0.8
HALO = 4
TILE_AXES = ("z", "y", "core")
ROWS = 16
VMEM = pl.BlockSpec(memory_space=pltpu.VMEM)
HBM = pl.BlockSpec(memory_space=pltpu.HBM)


def position():
    z, y, core = (lax.axis_index(a) for a in TILE_AXES)
    tile = (z * lax.axis_size("y") + y) * lax.axis_size("core") + core
    return lax.axis_index("group"), tile, core, y


def call(kernel, out_shape, in_specs, scratch=(), name=None, aliases=None):
    outs = jax.tree.map(lambda _: VMEM, out_shape)
    return pl.pallas_call(
        kernel,
        out_shape=out_shape,
        in_specs=in_specs,
        out_specs=outs,
        scratch_shapes=list(scratch),
        name=name,
        input_output_aliases=aliases or {},
        compiler_params=pltpu.CompilerParams(vmem_limit_bytes=24 * 1024 * 1024),
    )


def f32(*shape):
    return jax.ShapeDtypeStruct(shape, jnp.float32)


def low_half(shape):
    return lax.broadcasted_iota(jnp.int32, shape, 0) < shape[0] // 2


def row_tiles(r, source):
    low = low_half(r.shape)
    half = r.shape[0] // 2
    return jnp.where(low, r, pltpu.roll(source, half, 0)), jnp.where(low, pltpu.roll(r, half, 0), source)


def rows_kernel(
    chunks, table_hbm, facies_hbm, source_hbm, r_ref, source_ref, near_ref, far_ref,
    table_ref, facies_ref, table_sem, sems,
):
    core = position()[2]
    planes, rows, depth = facies_ref.shape
    kinds = table_ref.shape[0]
    first = core == 0
    step = planes // chunks
    table = pltpu.make_async_copy(table_hbm, table_ref, table_sem)
    table.start()
    copies = []
    for chunk in range(chunks):
        part = pl.ds(chunk * step, step)
        pair = (
            pltpu.make_async_copy(facies_hbm.at[part], facies_ref.at[part], sems.at[0, chunk]),
            pltpu.make_async_copy(source_hbm.at[part], source_ref.at[part], sems.at[1, chunk]),
        )
        for copy in pair:
            copy.start()
        copies.append(pair)
    table.wait()

    for chunk in range(chunks):
        for copy in copies[chunk]:
            copy.wait()

        def body(x, carry):
            facies = facies_ref[x]
            perm = jnp.full((rows, depth), table_ref[0], jnp.float32)
            for kind in range(1, kinds):
                perm = jnp.where(facies == kind, table_ref[kind], perm)
            r = 1.0 / perm
            source = source_ref[x]
            r_ref[x] = r
            begin, end = row_tiles(r, source)
            near_ref[x] = jnp.where(first, end, begin)
            far_ref[x] = jnp.where(first, begin, end)
            return carry

        lax.fori_loop(chunk * step, (chunk + 1) * step, body, 0, unroll=8)


def halo_rows(near, far, core, tile, tiles):
    low = low_half(near.shape)
    first = core == 0
    after = jnp.where(first, near, far)
    before = jnp.where(first, far, near)
    half = near.shape[0] // 2
    r = jnp.where(low, after, pltpu.roll(before, half, 0))
    source = jnp.where(low, pltpu.roll(after, half, 0), before)
    absent = (low & (tile == tiles - 1)) | (~low & (tile == 0))
    return jnp.where(absent, 1.0, r), jnp.where(absent, 0.0, source)


def planes_kernel(r_ref, source_ref, near_ref, begin_ref, end_ref):
    planes = r_ref.shape[0]
    for d in range(HALO):
        for out, x in ((begin_ref, d), (end_ref, planes - 1 - d)):
            out[d] = r_ref[x]
            if d < HALO - 1:
                out[4 + d] = near_ref[x]
                out[7 + d] = source_ref[x]


def corners_kernel(begin_ref, end_ref, out_ref):
    first = position()[2] == 0
    for side, recv in enumerate((begin_ref, end_ref)):
        for d in range(HALO - 1):
            begin, end = row_tiles(recv[d], recv[7 + d])
            out_ref[3 * side + d] = jnp.where(first, begin, end)


class Walls:
    def __init__(self, planes, rows, depth):
        self.group, self.tile, self.core, self.y = position()
        self.groups = lax.axis_size("group")
        self.tiles = lax.axis_size("z") * lax.axis_size("y") * lax.axis_size("core")
        self.planes, self.rows, self.depth = planes, rows, depth
        self.row = lax.broadcasted_iota(jnp.int32, (ROWS, depth), 0)
        column = lax.broadcasted_iota(jnp.int32, (ROWS, depth), 1)
        top = (self.row == ROWS - 1) & (self.tile == 0)
        self.in_y = top | ((self.row == rows - 1) & (self.tile == self.tiles - 1))
        self.in_z = column == depth - 1

    def faces(self, storage, x, before, tx, rr_ref, ss_ref, refs):
        ty_ref, tz_ref, w_ref, ws_ref = refs
        r = rr_ref[x]
        ty = jnp.where(self.in_y, 0.0, 2.0 / (r + pltpu.roll(r, ROWS - 1, 0)))
        tz = jnp.where(self.in_z, 0.0, 2.0 / (r + pltpu.roll(r, self.depth - 1, 1)))
        diagonal = storage + tx + before + ty + pltpu.roll(ty, 1, 0) + tz + pltpu.roll(tz, 1, 1)
        w = RELAX / diagonal
        ty_ref[x] = ty
        tz_ref[x] = tz
        w_ref[x] = w
        ws_ref[x] = w * ss_ref[x]


def middle_kernel(
    storage,
    r_ref, source_ref, near_ref, far_ref,
    part_ref, v_ref, tx_ref, ty_ref, tz_ref, w_ref, ws_ref, rr_ref, ss_ref,
):
    planes, rows, depth = r_ref.shape
    walls = Walls(planes, rows, depth)
    first, last = HALO, HALO + planes - 1

    def gather_rows(x, carry):
        side_r, side_source = halo_rows(near_ref[x], far_ref[x], walls.core, walls.tile, walls.tiles)
        rr_ref[HALO + x, 0:rows] = r_ref[x]
        rr_ref[HALO + x, rows:ROWS] = side_r
        ss_ref[HALO + x, 0:rows] = source_ref[x]
        ss_ref[HALO + x, rows:ROWS] = side_source
        return carry

    lax.fori_loop(0, planes, gather_rows, 0, unroll=16)
    refs = ty_ref, tz_ref, w_ref, ws_ref

    def faces(x, before):
        tx = 2.0 / (rr_ref[x] + rr_ref[x + 1])
        tx_ref[x] = tx
        walls.faces(storage, x, before, tx, rr_ref, ss_ref, refs)
        return tx

    start = 2.0 / (rr_ref[first] + rr_ref[first + 1])
    tx_ref[first] = start
    lax.fori_loop(first + 1, last, faces, start, unroll=16)

    def second(x, carry):
        total, y_flux, link_y, before = carry
        ty = ty_ref[x]
        v, ahead = relax(
            ws_ref[x], ws_ref[x + 1], before, tx_ref[x], ty, tz_ref[x], w_ref[x], ws_ref[x], depth
        )
        v_ref[x] = v
        total = total + ss_ref[x, 0:rows] - storage * v[0:rows]
        y_flux = y_flux + ty * (v - pltpu.roll(v, ROWS - 1, 0))
        return total, y_flux, link_y + ty[0:rows], ahead

    zeros = jnp.zeros((rows, depth), jnp.float32)
    carry = zeros, jnp.zeros((ROWS, depth), jnp.float32), zeros, start_flow(tx_ref, ws_ref, first + 1)
    total, y_flux, link_y, _ = lax.fori_loop(first + 2, last - 1, second, carry, unroll=15)
    part_ref[0:rows] = total
    part_ref[rows : rows + ROWS] = y_flux
    part_ref[rows + ROWS :] = link_y


def start_flow(tx_ref, h_ref, x):
    return tx_ref[x] * h_ref[x]


def edges_kernel(
    storage,
    begin_ref, end_ref, corner_ref,
    part_ref, v_in, tx_in, ty_in, tz_in, w_in, ws_in, rr_in, ss_in,
    sums_ref, v_ref, tx_ref, ty_ref, tz_ref, w_ref, ws_ref, rr_ref, ss_ref,
):
    wide, _, depth = v_ref.shape
    planes, rows = wide - 2 * HALO, begin_ref.shape[1]
    walls = Walls(planes, rows, depth)
    first, last = HALO, HALO + planes - 1
    group, row = walls.group, walls.row
    ones = jnp.ones((rows, depth), jnp.float32)
    zeros = jnp.zeros((rows, depth), jnp.float32)
    for d in range(HALO):
        for side, recv, x, there in (
            (1, end_ref, first - 1 - d, group > 0),
            (0, begin_ref, last + 1 + d, group < walls.groups - 1),
        ):
            side_r, side_source, own_source = ones, zeros, zeros
            if d < HALO - 1:
                far = corner_ref[3 * side + d]
                side_r, side_source = halo_rows(recv[4 + d], far, walls.core, walls.tile, walls.tiles)
                own_source = recv[7 + d]
            rr_ref[x, 0:rows] = jnp.where(there, recv[d], 1.0)
            rr_ref[x, rows:ROWS] = jnp.where(there, side_r, 1.0)
            ss_ref[x, 0:rows] = jnp.where(there, own_source, 0.0)
            ss_ref[x, rows:ROWS] = jnp.where(there, side_source, 0.0)

    refs = ty_ref, tz_ref, w_ref, ws_ref
    for begin, end in ((1, first), (last, wide - 2)):
        before = tx_ref[last - 1] if begin == last else 2.0 / (rr_ref[0] + rr_ref[1])
        for x in range(begin, end + 1):
            tx = 2.0 / (rr_ref[x] + rr_ref[x + 1])
            if x == first - 1:
                tx = jnp.where(group == 0, 0.0, tx)
            if x == last:
                tx = jnp.where(group == walls.groups - 1, 0.0, tx)
            tx_ref[x] = tx
            walls.faces(storage, x, before, tx, rr_ref, ss_ref, refs)
            before = tx

    total = part_ref[0:rows]
    y_flux = part_ref[rows : rows + ROWS]
    link_y = part_ref[rows + ROWS :]
    for begin, end in ((2, first + 1), (last - 1, wide - 3)):
        before = start_flow(tx_ref, ws_ref, begin - 1)
        for x in range(begin, end + 1):
            ty = ty_ref[x]
            v, before = relax(
                ws_ref[x], ws_ref[x + 1], before, tx_ref[x], ty, tz_ref[x], w_ref[x], ws_ref[x], depth
            )
            v_ref[x] = v
            if first <= x <= last:
                total = total + ss_ref[x, 0:rows] - storage * v[0:rows]
                y_flux = y_flux + ty * (v - pltpu.roll(v, ROWS - 1, 0))
                link_y = link_y + ty[0:rows]

    out_left = tx_ref[first - 1, 0:rows] * (v_ref[first, 0:rows] - v_ref[first - 1, 0:rows])
    out_right = tx_ref[last, 0:rows] * (v_ref[last, 0:rows] - v_ref[last + 1, 0:rows])
    side = jnp.where(row == ROWS - 1, y_flux, jnp.where(row == rows - 1, -y_flux, 0.0))
    rhs = total - out_left - out_right + side[0:rows] + side[rows:ROWS]
    rhs = jnp.sum(rhs, keepdims=True)
    link_x = jnp.sum(tx_ref[last, 0:rows], keepdims=True)
    link_y = jnp.sum(jnp.where(row[0:rows] == rows - 1, link_y, 0.0), keepdims=True)
    lane = lax.broadcasted_iota(jnp.int32, (1, 128), 1) - (32 * group + 4 * walls.y)
    packed = jnp.where(lane == 0, rhs, 0.0) + jnp.where(lane == 1, link_x, 0.0)
    packed = packed + jnp.where(lane == 2, link_y, 0.0)
    for peer in range(sums_ref.shape[0]):
        sums_ref[peer] = packed


def relax(h, h_next, before, tx, ty, tz, w, ws, depth):
    ahead = tx * h
    flow = before + tx * h_next
    flow = flow + ty * pltpu.roll(h, h.shape[0] - 1, 0) + pltpu.roll(ty * h, 1, 0)
    flow = flow + tz * pltpu.roll(h, depth - 1, 1) + pltpu.roll(tz * h, 1, 1)
    return (1.0 - RELAX) * h + ws + w * flow, ahead


def merge_kernel(part_ref, out_ref):
    total = part_ref[0]
    for peer in range(1, part_ref.shape[0]):
        total = total + part_ref[peer]
    for peer in range(out_ref.shape[0]):
        out_ref[peer] = total


def before_by(pair, stride):
    even, odd = pair
    length = even.shape[0]
    if stride == 1:
        return pltpu.roll(odd, 1, 0), even
    shift = stride // 2
    return pltpu.roll(even, shift, 0), pltpu.roll(odd, shift, 0)


def after_by(pair, stride):
    even, odd = pair
    length = even.shape[0]
    if stride == 1:
        return odd, pltpu.roll(even, length - 1, 0)
    shift = length - stride // 2
    return pltpu.roll(even, shift, 0), pltpu.roll(odd, shift, 0)


def each(fn, *pairs):
    return tuple(fn(*values) for values in zip(*pairs, strict=True))


def coarse_solve(sums_ref, store_brick, levels):
    lines = sums_ref.shape[0] // 2
    lanes = sums_ref.shape[2]
    y_lane = lax.broadcasted_iota(jnp.int32, (8, lanes), 1) // 4 % 8
    own_y = y_lane == lax.broadcasted_iota(jnp.int32, (8, lanes), 0)

    def unpack(line):
        line = jnp.where(own_y, jnp.broadcast_to(line, (8, lanes)), 0.0)
        for shift in (16, 8, 4):
            line = line + pltpu.roll(line, lanes - shift, 1)
        return line

    rhs = tuple(
        jnp.concatenate([unpack(sums_ref[2 * z + core]) for z in range(lines)], axis=0)
        for core in range(2)
    )
    link_x = each(lambda a: pltpu.roll(a, lanes - 1, 1), rhs)
    link_y = each(lambda a: pltpu.roll(a, lanes - 2, 1), rhs)
    link_x_before = each(lambda a: pltpu.roll(a, 32, 1), link_x)
    link_y_before = before_by(link_y, 1)
    diagonal = each(lambda a, b, c, d: store_brick + a + b + c + d, link_x, link_x_before, link_y, link_y_before)
    upper = each(lambda a: -a, link_y)
    alphas, gammas = [], []
    for level in range(levels):
        stride = 1 << level
        inverse = each(lambda d: 1.0 / d, diagonal)
        ratio = each(lambda u, i: -u * i, upper, inverse)
        alpha = before_by(ratio, stride)
        gamma = each(lambda u, i: -u * i, upper, after_by(inverse, stride))
        low = before_by(each(lambda q, u: q * u, ratio, upper), stride)
        diagonal = each(lambda d, a, g, u: d + a + g * u, diagonal, low, gamma, upper)
        upper = each(lambda g, u: g * u, gamma, after_by(upper, stride))
        alphas.append(alpha)
        gammas.append(gamma)
    inverse = each(lambda d: 1.0 / d, diagonal)
    correction = None
    for sweep_no in range(COARSE_ITERS):
        now = rhs
        if sweep_no:
            now = each(
                lambda r, a, b, c: r + a * pltpu.roll(c, 32, 1) + b * pltpu.roll(c, lanes - 32, 1),
                rhs, link_x_before, link_x, correction,
            )
        for level in range(levels):
            stride = 1 << level
            now = each(
                lambda n, a, p, g, q: n + a * p + g * q,
                now, alphas[level], before_by(now, stride), gammas[level], after_by(now, stride),
            )
        correction = each(lambda n, i: n * i, now, inverse)
    return correction


def last_kernel(
    store_brick, levels,
    sums_ref, v_ref, tx_ref, ty_ref, tz_ref, w_ref, ws_ref,
    out_ref,
    lines_ref, h_ref, g_ref,
):
    group, tile, core, _ = position()
    planes, rows, depth = out_ref.shape
    even, odd = coarse_solve(sums_ref, store_brick, levels)
    length = even.shape[0]
    for parity, line in ((0, even), (1, odd)):
        lines_ref[parity, 0:8] = jnp.zeros((8, line.shape[1]), jnp.float32)
        lines_ref[parity, 8 : 8 + length] = line
        lines_ref[parity, 8 + length : 16 + length] = jnp.zeros((8, line.shape[1]), jnp.float32)
    half = tile // 2
    here = lines_ref[core, pl.ds(8 + half, 1), :]
    ahead = lines_ref[1 - core, pl.ds(8 + half + core, 1), :]
    behind = lines_ref[1 - core, pl.ds(7 + half + core, 1), :]
    lane = lax.broadcasted_iota(jnp.int32, here.shape, 1)
    row = lax.broadcasted_iota(jnp.int32, (ROWS, depth), 0)

    def shift_of(offset):
        own, up, down = (
            jnp.sum(jnp.where(lane == 32 * (group + offset), line, 0.0), keepdims=True)
            for line in (here, ahead, behind)
        )
        return jnp.where(row < rows, own, jnp.where(row < rows + HALO, up, down))

    shifts = [shift_of(offset) for offset in (-1, 0, 1)]
    for x in (2, 3):
        h_ref[x] = v_ref[x] + shifts[0]
        h_ref[HALO + planes + x - 2] = v_ref[HALO + planes + x - 2] + shifts[2]
    middle = shifts[1]

    def lift(x, carry):
        h_ref[x] = v_ref[x] + middle
        return carry

    lax.fori_loop(HALO, HALO + planes, lift, 0, unroll=4)

    def third(x, before):
        v, ahead = relax(
            h_ref[x], h_ref[x + 1], before, tx_ref[x], ty_ref[x], tz_ref[x], w_ref[x], ws_ref[x], depth
        )
        g_ref[x] = v
        return ahead

    lax.fori_loop(HALO - 1, HALO + planes + 1, third, tx_ref[HALO - 2] * h_ref[HALO - 2], unroll=16)

    def fourth(x, before):
        h = g_ref[x]
        h_own = h[0:rows]
        tx = tx_ref[x, 0:rows]
        tz = tz_ref[x, 0:rows]
        ty = ty_ref[x]
        ahead = tx * h_own
        flow = before + tx * g_ref[x + 1, 0:rows]
        flow = flow + (ty * pltpu.roll(h, ROWS - 1, 0) + pltpu.roll(ty * h, 1, 0))[0:rows]
        flow = flow + tz * pltpu.roll(h_own, depth - 1, 1) + pltpu.roll(tz * h_own, 1, 1)
        out_ref[x - HALO] = (1.0 - RELAX) * h_own + ws_ref[x, 0:rows] + w_ref[x, 0:rows] * flow
        return ahead

    first = tx_ref[HALO - 1, 0:rows] * g_ref[HALO - 1, 0:rows]
    lax.fori_loop(HALO, HALO + planes, fourth, first, unroll=16)


def spread(block, axes):
    return lax.all_to_all(block, axes, 0, 0)


def on_device(facies, perm_table, source):
    planes, rows, depth = source.shape
    storage = 0.01 / rows
    groups = lax.axis_size("group")
    z_size, y_size, cores = (lax.axis_size(a) for a in TILE_AXES)
    tiles = z_size * y_size * cores
    brick = f32(planes, rows, depth)
    chunks = 4
    r, source, near, far = call(
        functools.partial(rows_kernel, chunks),
        (brick,) * 4,
        [HBM] * 3,
        [
            pltpu.SMEM(perm_table.shape, jnp.float32),
            pltpu.VMEM(source.shape, jnp.int32),
            pltpu.SemaphoreType.DMA,
            pltpu.SemaphoreType.DMA((2, chunks)),
        ],
        name="rows",
    )(*(pltpu.with_memory_space_constraint(a, pltpu.HBM) for a in (perm_table, facies, source)))
    pairs = [p for i in range(1, tiles - 1, 2) for p in ((i, i + 1), (i + 1, i))]
    far = lax.ppermute(far, TILE_AXES, pairs)
    near = lax.ppermute(near, "core", [(0, 1), (1, 0)])
    slab = f32(10, rows, depth)
    begin, end = call(planes_kernel, (slab, slab), [VMEM] * 3, name="planes")(r, source, near)
    end = lax.ppermute(end, "group", [(i, i + 1) for i in range(groups - 1)])
    begin = lax.ppermute(begin, "group", [(i + 1, i) for i in range(groups - 1)])
    corner = call(corners_kernel, f32(6, rows, depth), [VMEM] * 2, name="corners")(begin, end)
    corner = lax.ppermute(corner, TILE_AXES, pairs)
    wide = f32(planes + 2 * HALO, ROWS, depth)
    scratch = [pltpu.VMEM(wide.shape, jnp.float32)]
    part, *fields = call(
        functools.partial(middle_kernel, storage),
        (f32(2 * rows + ROWS, depth),) + (wide,) * 8,
        [VMEM] * 4,
        name="middle",
    )(r, source, near, far)
    sums, *fields = call(
        functools.partial(edges_kernel, storage),
        (f32(groups * y_size, 1, 128),) + (wide,) * 8,
        [VMEM] * 12,
        name="edges",
        aliases={4 + i: 1 + i for i in range(8)},
    )(begin, end, corner, part, *fields)
    fields = fields[:6]
    sums = spread(sums, ("group", "y"))
    sums = call(merge_kernel, f32(z_size * cores, 1, 128), [VMEM], name="merge")(sums)
    sums = spread(sums, ("z", "core"))
    length = z_size * y_size
    return call(
        functools.partial(last_kernel, storage * planes * rows * depth, tiles.bit_length() - 1),
        brick,
        [VMEM] * 7,
        [pltpu.VMEM((2, length + 16, 128), jnp.float32)] + scratch * 2,
        name="last",
    )(sums, *fields)


def solution(mesh):
    groups, tiles = mesh.shape["group"], mesh.shape["tile"]
    chips = Mesh(mesh.devices.reshape(groups, tiles // 16, 8, 2), ("group",) + TILE_AXES)
    cells = P("group", TILE_AXES, None)
    return jax.shard_map(
        on_device, mesh=chips, in_specs=(cells, P(), cells), out_specs=cells, check_vma=False
    )
```

```python
import functools

import jax
import jax.numpy as jnp
from jax import lax
from jax.experimental import pallas as pl
from jax.experimental.pallas import tpu as pltpu
from jax.sharding import Mesh
from jax.sharding import PartitionSpec as P

COARSE_ITERS = 3
RELAX = 0.8
HALO = 4
TILE_AXES = ("z", "y", "core")
ROWS = 16
VMEM = pl.BlockSpec(memory_space=pltpu.VMEM)
HBM = pl.BlockSpec(memory_space=pltpu.HBM)


def position():
    z, y, core = (lax.axis_index(a) for a in TILE_AXES)
    tile = (z * lax.axis_size("y") + y) * lax.axis_size("core") + core
    return lax.axis_index("group"), tile, core, y


def call(kernel, out_shape, in_specs, scratch=(), name=None, aliases=None, out_spec=VMEM):
    outs = jax.tree.map(lambda _: out_spec, out_shape)
    return pl.pallas_call(
        kernel,
        out_shape=out_shape,
        in_specs=in_specs,
        out_specs=outs,
        scratch_shapes=list(scratch),
        name=name,
        input_output_aliases=aliases or {},
        compiler_params=pltpu.CompilerParams(vmem_limit_bytes=24 * 1024 * 1024),
    )


def f32(*shape):
    return jax.ShapeDtypeStruct(shape, jnp.float32)


def low_half(shape):
    return lax.broadcasted_iota(jnp.int32, shape, 0) < shape[0] // 2


def row_tiles(r, source):
    low = low_half(r.shape)
    half = r.shape[0] // 2
    return jnp.where(low, r, pltpu.roll(source, half, 0)), jnp.where(low, pltpu.roll(r, half, 0), source)


def rows_kernel(
    chunks, table_hbm, facies_hbm, source_hbm, r_ref, source_ref, near_ref, far_ref,
    table_ref, facies_ref, table_sem, sems,
):
    core = position()[2]
    planes, rows, depth = facies_ref.shape
    kinds = table_ref.shape[0]
    first = core == 0
    step = planes // chunks
    table = pltpu.make_async_copy(table_hbm, table_ref, table_sem)
    table.start()
    copies = []
    for chunk in range(chunks):
        part = pl.ds(chunk * step, step)
        pair = (
            pltpu.make_async_copy(facies_hbm.at[part], facies_ref.at[part], sems.at[0, chunk]),
            pltpu.make_async_copy(source_hbm.at[part], source_ref.at[part], sems.at[1, chunk]),
        )
        for copy in pair:
            copy.start()
        copies.append(pair)
    table.wait()

    for chunk in range(chunks):
        for copy in copies[chunk]:
            copy.wait()

        def body(x, carry):
            facies = facies_ref[x]
            perm = jnp.full((rows, depth), table_ref[0], jnp.float32)
            for kind in range(1, kinds):
                perm = jnp.where(facies == kind, table_ref[kind], perm)
            r = 1.0 / perm
            source = source_ref[x]
            r_ref[x] = r
            begin, end = row_tiles(r, source)
            near_ref[x] = jnp.where(first, end, begin)
            far_ref[x] = jnp.where(first, begin, end)
            return carry

        lax.fori_loop(chunk * step, (chunk + 1) * step, body, 0, unroll=8)


def halo_rows(near, far, core, tile, tiles):
    low = low_half(near.shape)
    first = core == 0
    after = jnp.where(first, near, far)
    before = jnp.where(first, far, near)
    half = near.shape[0] // 2
    r = jnp.where(low, after, pltpu.roll(before, half, 0))
    source = jnp.where(low, pltpu.roll(after, half, 0), before)
    absent = (low & (tile == tiles - 1)) | (~low & (tile == 0))
    return jnp.where(absent, 1.0, r), jnp.where(absent, 0.0, source)


def planes_kernel(r_ref, source_ref, near_ref, begin_ref, end_ref):
    planes = r_ref.shape[0]
    for d in range(HALO):
        for out, x in ((begin_ref, d), (end_ref, planes - 1 - d)):
            out[d] = r_ref[x]
            if d < HALO - 1:
                out[4 + d] = near_ref[x]
                out[7 + d] = source_ref[x]


def corners_kernel(begin_ref, end_ref, out_ref):
    first = position()[2] == 0
    for side, recv in enumerate((begin_ref, end_ref)):
        for d in range(HALO - 1):
            begin, end = row_tiles(recv[d], recv[7 + d])
            out_ref[3 * side + d] = jnp.where(first, begin, end)


class Walls:
    def __init__(self, planes, rows, depth):
        self.group, self.tile, self.core, self.y = position()
        self.groups = lax.axis_size("group")
        self.tiles = lax.axis_size("z") * lax.axis_size("y") * lax.axis_size("core")
        self.planes, self.rows, self.depth = planes, rows, depth
        self.row = lax.broadcasted_iota(jnp.int32, (ROWS, depth), 0)
        column = lax.broadcasted_iota(jnp.int32, (ROWS, depth), 1)
        top = (self.row == ROWS - 1) & (self.tile == 0)
        self.in_y = top | ((self.row == rows - 1) & (self.tile == self.tiles - 1))
        self.in_z = column == depth - 1

    def faces(self, storage, x, before, rr_ref, ss_ref, refs, x_wall=None):
        tx_ref, ty_ref, tz_ref, w_ref, ws_ref = refs
        r = rr_ref[x]
        over_x = r + rr_ref[x + 1]
        over_y = r + pltpu.roll(r, ROWS - 1, 0)
        over_z = r + pltpu.roll(r, self.depth - 1, 1)
        over_xy = over_x * over_y
        share = 2.0 / (over_xy * over_z)
        rest = share * over_z
        tx = rest * over_y
        if x_wall is not None:
            tx = jnp.where(x_wall, 0.0, tx)
        ty = jnp.where(self.in_y, 0.0, rest * over_x)
        tz = jnp.where(self.in_z, 0.0, share * over_xy)
        diagonal = storage + tx + before + ty + pltpu.roll(ty, 1, 0) + tz + pltpu.roll(tz, 1, 1)
        w = RELAX / diagonal
        tx_ref[x] = tx
        ty_ref[x] = ty
        tz_ref[x] = tz
        w_ref[x] = w
        ws_ref[x] = w * ss_ref[x]
        return tx


def middle_kernel(
    storage,
    r_ref, source_ref, near_ref, far_ref,
    part_ref, v_ref, tx_ref, ty_ref, tz_ref, w_ref, ws_ref, rr_ref, ss_ref,
):
    planes, rows, depth = r_ref.shape
    walls = Walls(planes, rows, depth)
    first, last = HALO, HALO + planes - 1

    def gather_rows(x, carry):
        side_r, side_source = halo_rows(near_ref[x], far_ref[x], walls.core, walls.tile, walls.tiles)
        rr_ref[HALO + x, 0:rows] = r_ref[x]
        rr_ref[HALO + x, rows:ROWS] = side_r
        ss_ref[HALO + x, 0:rows] = source_ref[x]
        ss_ref[HALO + x, rows:ROWS] = side_source
        return carry

    lax.fori_loop(0, planes, gather_rows, 0, unroll=16)
    refs = tx_ref, ty_ref, tz_ref, w_ref, ws_ref

    def faces(x, before):
        return walls.faces(storage, x, before, rr_ref, ss_ref, refs)

    start = 2.0 / (rr_ref[first] + rr_ref[first + 1])
    tx_ref[first] = start
    lax.fori_loop(first + 1, last, faces, start, unroll=31)

    def second(x, carry):
        total, y_flux, link_y, before = carry
        ty = ty_ref[x]
        v, ahead = relax(
            ws_ref[x], ws_ref[x + 1], before, tx_ref[x], ty, tz_ref[x], w_ref[x], ws_ref[x], depth
        )
        v_ref[x] = v
        total = total + ss_ref[x, 0:rows] - storage * v[0:rows]
        y_flux = y_flux + ty * (v - pltpu.roll(v, ROWS - 1, 0))
        return total, y_flux, link_y + ty[0:rows], ahead

    zeros = jnp.zeros((rows, depth), jnp.float32)
    carry = zeros, jnp.zeros((ROWS, depth), jnp.float32), zeros, start_flow(tx_ref, ws_ref, first + 1)
    total, y_flux, link_y, _ = lax.fori_loop(first + 2, last - 1, second, carry, unroll=15)
    part_ref[0:rows] = total
    part_ref[rows : rows + ROWS] = y_flux
    part_ref[rows + ROWS :] = link_y


def start_flow(tx_ref, h_ref, x):
    return tx_ref[x] * h_ref[x]


def edges_kernel(
    storage,
    begin_ref, end_ref, corner_ref,
    part_ref, v_in, tx_in, ty_in, tz_in, w_in, ws_in, rr_in, ss_in,
    sums_ref, v_ref, tx_ref, ty_ref, tz_ref, w_ref, ws_ref, rr_ref, ss_ref,
):
    wide, _, depth = v_ref.shape
    planes, rows = wide - 2 * HALO, begin_ref.shape[1]
    walls = Walls(planes, rows, depth)
    first, last = HALO, HALO + planes - 1
    group, row = walls.group, walls.row
    ones = jnp.ones((rows, depth), jnp.float32)
    zeros = jnp.zeros((rows, depth), jnp.float32)
    for d in range(HALO):
        for side, recv, x, there in (
            (1, end_ref, first - 1 - d, group > 0),
            (0, begin_ref, last + 1 + d, group < walls.groups - 1),
        ):
            side_r, side_source, own_source = ones, zeros, zeros
            if d < HALO - 1:
                far = corner_ref[3 * side + d]
                side_r, side_source = halo_rows(recv[4 + d], far, walls.core, walls.tile, walls.tiles)
                own_source = recv[7 + d]
            rr_ref[x, 0:rows] = jnp.where(there, recv[d], 1.0)
            rr_ref[x, rows:ROWS] = jnp.where(there, side_r, 1.0)
            ss_ref[x, 0:rows] = jnp.where(there, own_source, 0.0)
            ss_ref[x, rows:ROWS] = jnp.where(there, side_source, 0.0)

    refs = tx_ref, ty_ref, tz_ref, w_ref, ws_ref
    for begin, end in ((1, first), (last, wide - 2)):
        before = tx_ref[last - 1] if begin == last else 2.0 / (rr_ref[0] + rr_ref[1])
        for x in range(begin, end + 1):
            wall = {first - 1: group == 0, last: group == walls.groups - 1}.get(x)
            before = walls.faces(storage, x, before, rr_ref, ss_ref, refs, wall)

    total = part_ref[0:rows]
    y_flux = part_ref[rows : rows + ROWS]
    link_y = part_ref[rows + ROWS :]
    for begin, end in ((2, first + 1), (last - 1, wide - 3)):
        before = start_flow(tx_ref, ws_ref, begin - 1)
        for x in range(begin, end + 1):
            ty = ty_ref[x]
            v, before = relax(
                ws_ref[x], ws_ref[x + 1], before, tx_ref[x], ty, tz_ref[x], w_ref[x], ws_ref[x], depth
            )
            v_ref[x] = v
            if first <= x <= last:
                total = total + ss_ref[x, 0:rows] - storage * v[0:rows]
                y_flux = y_flux + ty * (v - pltpu.roll(v, ROWS - 1, 0))
                link_y = link_y + ty[0:rows]

    out_left = tx_ref[first - 1, 0:rows] * (v_ref[first, 0:rows] - v_ref[first - 1, 0:rows])
    out_right = tx_ref[last, 0:rows] * (v_ref[last, 0:rows] - v_ref[last + 1, 0:rows])
    side = jnp.where(row == ROWS - 1, y_flux, jnp.where(row == rows - 1, -y_flux, 0.0))
    rhs = total - out_left - out_right + side[0:rows] + side[rows:ROWS]
    rhs = jnp.sum(rhs, keepdims=True)
    link_x = jnp.sum(tx_ref[last, 0:rows], keepdims=True)
    link_y = jnp.sum(jnp.where(row[0:rows] == rows - 1, link_y, 0.0), keepdims=True)
    lane = lax.broadcasted_iota(jnp.int32, (1, 128), 1) - (32 * group + 4 * walls.y)
    packed = jnp.where(lane == 0, rhs, 0.0) + jnp.where(lane == 1, link_x, 0.0)
    packed = packed + jnp.where(lane == 2, link_y, 0.0)
    for peer in range(sums_ref.shape[0]):
        sums_ref[peer] = packed


def relax(h, h_next, before, tx, ty, tz, w, ws, depth):
    ahead = tx * h
    flow = before + tx * h_next
    flow = flow + ty * pltpu.roll(h, h.shape[0] - 1, 0) + pltpu.roll(ty * h, 1, 0)
    flow = flow + tz * pltpu.roll(h, depth - 1, 1) + pltpu.roll(tz * h, 1, 1)
    return (1.0 - RELAX) * h + ws + w * flow, ahead


def merge_kernel(part_ref, out_ref):
    total = part_ref[0]
    for peer in range(1, part_ref.shape[0]):
        total = total + part_ref[peer]
    for peer in range(out_ref.shape[0]):
        out_ref[peer] = total


def before_by(pair, stride):
    even, odd = pair
    length = even.shape[0]
    if stride == 1:
        return pltpu.roll(odd, 1, 0), even
    shift = stride // 2
    return pltpu.roll(even, shift, 0), pltpu.roll(odd, shift, 0)


def after_by(pair, stride):
    even, odd = pair
    length = even.shape[0]
    if stride == 1:
        return odd, pltpu.roll(even, length - 1, 0)
    shift = length - stride // 2
    return pltpu.roll(even, shift, 0), pltpu.roll(odd, shift, 0)


def each(fn, *pairs):
    return tuple(fn(*values) for values in zip(*pairs, strict=True))


def coarse_solve(sums_ref, store_brick, levels):
    lines = sums_ref.shape[0] // 2
    lanes = sums_ref.shape[2]
    y_lane = lax.broadcasted_iota(jnp.int32, (8, lanes), 1) // 4 % 8
    own_y = y_lane == lax.broadcasted_iota(jnp.int32, (8, lanes), 0)

    def unpack(line):
        line = jnp.where(own_y, jnp.broadcast_to(line, (8, lanes)), 0.0)
        for shift in (16, 8, 4):
            line = line + pltpu.roll(line, lanes - shift, 1)
        return line

    rhs = tuple(
        jnp.concatenate([unpack(sums_ref[2 * z + core]) for z in range(lines)], axis=0)
        for core in range(2)
    )
    link_x = each(lambda a: pltpu.roll(a, lanes - 1, 1), rhs)
    link_y = each(lambda a: pltpu.roll(a, lanes - 2, 1), rhs)
    link_x_before = each(lambda a: pltpu.roll(a, 32, 1), link_x)
    link_y_before = before_by(link_y, 1)
    diagonal = each(lambda a, b, c, d: store_brick + a + b + c + d, link_x, link_x_before, link_y, link_y_before)
    upper = each(lambda a: -a, link_y)
    alphas, gammas = [], []
    for level in range(levels):
        stride = 1 << level
        inverse = each(lambda d: 1.0 / d, diagonal)
        ratio = each(lambda u, i: -u * i, upper, inverse)
        alpha = before_by(ratio, stride)
        gamma = each(lambda u, i: -u * i, upper, after_by(inverse, stride))
        low = before_by(each(lambda q, u: q * u, ratio, upper), stride)
        diagonal = each(lambda d, a, g, u: d + a + g * u, diagonal, low, gamma, upper)
        upper = each(lambda g, u: g * u, gamma, after_by(upper, stride))
        alphas.append(alpha)
        gammas.append(gamma)
    inverse = each(lambda d: 1.0 / d, diagonal)
    correction = None
    for sweep_no in range(COARSE_ITERS):
        now = rhs
        if sweep_no:
            now = each(
                lambda r, a, b, c: r + a * pltpu.roll(c, 32, 1) + b * pltpu.roll(c, lanes - 32, 1),
                rhs, link_x_before, link_x, correction,
            )
        for level in range(levels):
            stride = 1 << level
            now = each(
                lambda n, a, p, g, q: n + a * p + g * q,
                now, alphas[level], before_by(now, stride), gammas[level], after_by(now, stride),
            )
        correction = each(lambda n, i: n * i, now, inverse)
    return correction


def last_kernel(
    store_brick, levels, chunks,
    sums_ref, v_ref, tx_ref, ty_ref, tz_ref, w_ref, ws_ref,
    out_ref,
    lines_ref, g_ref, done_ref, sems,
):
    group, tile, core, _ = position()
    planes, rows, depth = out_ref.shape
    even, odd = coarse_solve(sums_ref, store_brick, levels)
    length = even.shape[0]
    for parity, line in ((0, even), (1, odd)):
        lines_ref[parity, 0:8] = jnp.zeros((8, line.shape[1]), jnp.float32)
        lines_ref[parity, 8 : 8 + length] = line
        lines_ref[parity, 8 + length : 16 + length] = jnp.zeros((8, line.shape[1]), jnp.float32)
    half = tile // 2
    here = lines_ref[core, pl.ds(8 + half, 1), :]
    ahead = lines_ref[1 - core, pl.ds(8 + half + core, 1), :]
    behind = lines_ref[1 - core, pl.ds(7 + half + core, 1), :]
    lane = lax.broadcasted_iota(jnp.int32, here.shape, 1)
    row = lax.broadcasted_iota(jnp.int32, (ROWS, depth), 0)

    def shift_of(offset):
        own, up, down = (
            jnp.sum(jnp.where(lane == 32 * (group + offset), line, 0.0), keepdims=True)
            for line in (here, ahead, behind)
        )
        return jnp.where(row < rows, own, jnp.where(row < rows + HALO, up, down))

    shifts = [shift_of(offset) for offset in (-1, 0, 1)]
    first, end = HALO, HALO + planes

    def third(x, h, h_next, before):
        v, ahead = relax(h, h_next, before, tx_ref[x], ty_ref[x], tz_ref[x], w_ref[x], ws_ref[x], depth)
        g_ref[x] = v
        return ahead

    def third_inside(x, carry):
        h, before = carry
        h_next = v_ref[x + 1] + shifts[1]
        return h_next, third(x, h, h_next, before)

    h = v_ref[first - 1] + shifts[0]
    h_next = v_ref[first] + shifts[1]
    before = third(first - 1, h, h_next, tx_ref[first - 2] * (v_ref[first - 2] + shifts[0]))
    h, before = lax.fori_loop(first, end - 1, third_inside, (h_next, before), unroll=31)
    h_next = v_ref[end] + shifts[2]
    before = third(end - 1, h, h_next, before)
    third(end, h_next, v_ref[end + 1] + shifts[2], before)

    def fourth(x, before):
        h = g_ref[x]
        h_own = h[0:rows]
        tx = tx_ref[x, 0:rows]
        tz = tz_ref[x, 0:rows]
        ty = ty_ref[x]
        ahead = tx * h_own
        flow = before + tx * g_ref[x + 1, 0:rows]
        flow = flow + (ty * pltpu.roll(h, ROWS - 1, 0) + pltpu.roll(ty * h, 1, 0))[0:rows]
        flow = flow + tz * pltpu.roll(h_own, depth - 1, 1) + pltpu.roll(tz * h_own, 1, 1)
        done_ref[x - HALO] = (1.0 - RELAX) * h_own + ws_ref[x, 0:rows] + w_ref[x, 0:rows] * flow
        return ahead

    before = tx_ref[first - 1, 0:rows] * g_ref[first - 1, 0:rows]
    step = planes // chunks
    copies = []
    for chunk in range(chunks):
        begin = first + chunk * step
        before = lax.fori_loop(begin, begin + step, fourth, before, unroll=16)
        part = pl.ds(chunk * step, step)
        copies.append(pltpu.make_async_copy(done_ref.at[part], out_ref.at[part], sems.at[chunk]))
        copies[-1].start()
    for copy in copies:
        copy.wait()


def spread(block, axes):
    return lax.all_to_all(block, axes, 0, 0)


def on_device(facies, perm_table, source):
    planes, rows, depth = source.shape
    storage = 0.01 / rows
    groups = lax.axis_size("group")
    z_size, y_size, cores = (lax.axis_size(a) for a in TILE_AXES)
    tiles = z_size * y_size * cores
    brick = f32(planes, rows, depth)
    chunks = 4
    r, source, near, far = call(
        functools.partial(rows_kernel, chunks),
        (brick,) * 4,
        [HBM] * 3,
        [
            pltpu.SMEM(perm_table.shape, jnp.float32),
            pltpu.VMEM(source.shape, jnp.int32),
            pltpu.SemaphoreType.DMA,
            pltpu.SemaphoreType.DMA((2, chunks)),
        ],
        name="rows",
    )(*(pltpu.with_memory_space_constraint(a, pltpu.HBM) for a in (perm_table, facies, source)))
    pairs = [p for i in range(1, tiles - 1, 2) for p in ((i, i + 1), (i + 1, i))]
    far = lax.ppermute(far, TILE_AXES, pairs)
    near = lax.ppermute(near, "core", [(0, 1), (1, 0)])
    slab = f32(10, rows, depth)
    begin, end = call(planes_kernel, (slab, slab), [VMEM] * 3, name="planes")(r, source, near)
    end = lax.ppermute(end, "group", [(i, i + 1) for i in range(groups - 1)])
    begin = lax.ppermute(begin, "group", [(i + 1, i) for i in range(groups - 1)])
    corner = call(corners_kernel, f32(6, rows, depth), [VMEM] * 2, name="corners")(begin, end)
    corner = lax.ppermute(corner, TILE_AXES, pairs)
    wide = f32(planes + 2 * HALO, ROWS, depth)
    part, *fields = call(
        functools.partial(middle_kernel, storage),
        (f32(2 * rows + ROWS, depth),) + (wide,) * 8,
        [VMEM] * 4,
        name="middle",
    )(r, source, near, far)
    sums, *fields = call(
        functools.partial(edges_kernel, storage),
        (f32(groups * y_size, 1, 128),) + (wide,) * 8,
        [VMEM] * 12,
        name="edges",
        aliases={4 + i: 1 + i for i in range(8)},
    )(begin, end, corner, part, *fields)
    fields = fields[:6]
    sums = spread(sums, ("group", "y"))
    sums = call(merge_kernel, f32(z_size * cores, 1, 128), [VMEM], name="merge")(sums)
    sums = spread(sums, ("z", "core"))
    length = z_size * y_size
    chunks = 4
    return call(
        functools.partial(last_kernel, storage * planes * rows * depth, tiles.bit_length() - 1, chunks),
        brick,
        [VMEM] * 7,
        [
            pltpu.VMEM((2, length + 16, 128), jnp.float32),
            pltpu.VMEM(wide.shape, jnp.float32),
            pltpu.VMEM(brick.shape, jnp.float32),
            pltpu.SemaphoreType.DMA((chunks,)),
        ],
        name="last",
        out_spec=HBM,
    )(sums, *fields)


def solution(mesh):
    groups, tiles = mesh.shape["group"], mesh.shape["tile"]
    chips = Mesh(mesh.devices.reshape(groups, tiles // 16, 8, 2), ("group",) + TILE_AXES)
    cells = P("group", TILE_AXES, None)
    return jax.shard_map(
        on_device, mesh=chips, in_specs=(cells, P(), cells), out_specs=cells, check_vma=False
    )
```

```python
import functools

import jax
import jax.numpy as jnp
from jax import lax
from jax.experimental import pallas as pl
from jax.experimental.pallas import tpu as pltpu
from jax.sharding import Mesh
from jax.sharding import PartitionSpec as P

COARSE_ITERS = 3
RELAX = 0.8
HALO = 4
TILE_AXES = ("z", "y", "core")
ROWS = 16
VMEM = pl.BlockSpec(memory_space=pltpu.VMEM)
HBM = pl.BlockSpec(memory_space=pltpu.HBM)


def position():
    z, y, core = (lax.axis_index(a) for a in TILE_AXES)
    tile = (z * lax.axis_size("y") + y) * lax.axis_size("core") + core
    return lax.axis_index("group"), tile, core, y


def call(kernel, out_shape, in_specs, scratch=(), name=None, aliases=None, out_spec=VMEM):
    outs = jax.tree.map(lambda _: out_spec, out_shape)
    return pl.pallas_call(
        kernel,
        out_shape=out_shape,
        in_specs=in_specs,
        out_specs=outs,
        scratch_shapes=list(scratch),
        name=name,
        input_output_aliases=aliases or {},
        compiler_params=pltpu.CompilerParams(vmem_limit_bytes=24 * 1024 * 1024),
    )


def f32(*shape):
    return jax.ShapeDtypeStruct(shape, jnp.float32)


def low_half(shape):
    return lax.broadcasted_iota(jnp.int32, shape, 0) < shape[0] // 2


def row_tiles(r, source):
    low = low_half(r.shape)
    half = r.shape[0] // 2
    return jnp.where(low, r, pltpu.roll(source, half, 0)), jnp.where(low, pltpu.roll(r, half, 0), source)


def rows_kernel(
    chunks, table_hbm, facies_hbm, source_hbm, r_ref, source_ref, near_ref, far_ref,
    table_ref, facies_ref, table_sem, sems,
):
    core = position()[2]
    planes, rows, depth = facies_ref.shape
    kinds = table_ref.shape[0]
    first = core == 0
    step = planes // chunks
    table = pltpu.make_async_copy(table_hbm, table_ref, table_sem)
    table.start()
    copies = []
    for chunk in range(chunks):
        part = pl.ds(chunk * step, step)
        pair = (
            pltpu.make_async_copy(facies_hbm.at[part], facies_ref.at[part], sems.at[0, chunk]),
            pltpu.make_async_copy(source_hbm.at[part], source_ref.at[part], sems.at[1, chunk]),
        )
        for copy in pair:
            copy.start()
        copies.append(pair)
    table.wait()

    for chunk in range(chunks):
        for copy in copies[chunk]:
            copy.wait()

        def body(x, carry):
            facies = facies_ref[x]
            perm = jnp.full((rows, depth), table_ref[0], jnp.float32)
            for kind in range(1, kinds):
                perm = jnp.where(facies == kind, table_ref[kind], perm)
            r = 1.0 / perm
            source = source_ref[x]
            r_ref[x] = r
            begin, end = row_tiles(r, source)
            near_ref[x] = jnp.where(first, end, begin)
            far_ref[x] = jnp.where(first, begin, end)
            return carry

        lax.fori_loop(chunk * step, (chunk + 1) * step, body, 0, unroll=8)
    for x in range(planes, far_ref.shape[0]):
        far_ref[x] = jnp.zeros((rows, depth), jnp.float32)


def halo_rows(near, far, core, tile, tiles):
    low = low_half(near.shape)
    first = core == 0
    after = jnp.where(first, near, far)
    before = jnp.where(first, far, near)
    half = near.shape[0] // 2
    r = jnp.where(low, after, pltpu.roll(before, half, 0))
    source = jnp.where(low, pltpu.roll(after, half, 0), before)
    absent = (low & (tile == tiles - 1)) | (~low & (tile == 0))
    return jnp.where(absent, 1.0, r), jnp.where(absent, 0.0, source)


def planes_kernel(r_ref, source_ref, begin_ref, end_ref):
    planes = r_ref.shape[0]
    for d in range(HALO):
        for out, x in ((begin_ref, d), (end_ref, planes - 1 - d)):
            out[d] = r_ref[x]
            if d < HALO - 1:
                out[4 + d] = source_ref[x]


def corners_kernel(begin_ref, end_ref, near_in, near_ref, corner_ref):
    first = position()[2] == 0
    count = HALO - 1
    own = near_ref.shape[0] - 2 * count
    for side, recv in enumerate((begin_ref, end_ref)):
        for d in range(count):
            begin, end = row_tiles(recv[d], recv[4 + d])
            near_ref[own + count * side + d] = jnp.where(first, end, begin)
            corner_ref[count * side + d] = jnp.where(first, begin, end)


class Walls:
    def __init__(self, planes, rows, depth):
        self.group, self.tile, self.core, self.y = position()
        self.groups = lax.axis_size("group")
        self.tiles = lax.axis_size("z") * lax.axis_size("y") * lax.axis_size("core")
        self.planes, self.rows, self.depth = planes, rows, depth
        self.row = lax.broadcasted_iota(jnp.int32, (ROWS, depth), 0)
        column = lax.broadcasted_iota(jnp.int32, (ROWS, depth), 1)
        top = (self.row == ROWS - 1) & (self.tile == 0)
        self.in_y = top | ((self.row == rows - 1) & (self.tile == self.tiles - 1))
        self.in_z = column == depth - 1

    def faces(self, storage, x, before, rr_ref, ss_ref, refs, x_wall=None):
        tx_ref, ty_ref, tz_ref, w_ref, ws_ref = refs
        r = rr_ref[x]
        over_x = r + rr_ref[x + 1]
        over_y = r + pltpu.roll(r, ROWS - 1, 0)
        over_z = r + pltpu.roll(r, self.depth - 1, 1)
        over_xy = over_x * over_y
        share = 2.0 / (over_xy * over_z)
        rest = share * over_z
        tx = rest * over_y
        if x_wall is not None:
            tx = jnp.where(x_wall, 0.0, tx)
        ty = jnp.where(self.in_y, 0.0, rest * over_x)
        tz = jnp.where(self.in_z, 0.0, share * over_xy)
        diagonal = storage + tx + before + ty + pltpu.roll(ty, 1, 0) + tz + pltpu.roll(tz, 1, 1)
        w = RELAX / diagonal
        tx_ref[x] = tx
        ty_ref[x] = ty
        tz_ref[x] = tz
        w_ref[x] = w
        ws_ref[x] = w * ss_ref[x]
        return tx


def middle_kernel(
    storage,
    r_ref, source_ref, near_ref, far_ref,
    part_ref, v_ref, tx_ref, ty_ref, tz_ref, w_ref, ws_ref, rr_ref, ss_ref,
):
    planes, rows, depth = r_ref.shape
    walls = Walls(planes, rows, depth)
    first, last = HALO, HALO + planes - 1

    def gather_rows(x, carry):
        side_r, side_source = halo_rows(near_ref[x], far_ref[x], walls.core, walls.tile, walls.tiles)
        rr_ref[HALO + x, 0:rows] = r_ref[x]
        rr_ref[HALO + x, rows:ROWS] = side_r
        ss_ref[HALO + x, 0:rows] = source_ref[x]
        ss_ref[HALO + x, rows:ROWS] = side_source
        return carry

    lax.fori_loop(0, planes, gather_rows, 0, unroll=16)
    refs = tx_ref, ty_ref, tz_ref, w_ref, ws_ref

    def faces(x, before):
        return walls.faces(storage, x, before, rr_ref, ss_ref, refs)

    start = 2.0 / (rr_ref[first] + rr_ref[first + 1])
    tx_ref[first] = start
    lax.fori_loop(first + 1, last, faces, start, unroll=31)

    def second(x, carry):
        total, y_flux, link_y, before = carry
        ty = ty_ref[x]
        v, ahead = relax(
            ws_ref[x], ws_ref[x + 1], before, tx_ref[x], ty, tz_ref[x], w_ref[x], ws_ref[x], depth
        )
        v_ref[x] = v
        total = total + ss_ref[x, 0:rows] - storage * v[0:rows]
        y_flux = y_flux + ty * (v - pltpu.roll(v, ROWS - 1, 0))
        return total, y_flux, link_y + ty[0:rows], ahead

    zeros = jnp.zeros((rows, depth), jnp.float32)
    carry = zeros, jnp.zeros((ROWS, depth), jnp.float32), zeros, start_flow(tx_ref, ws_ref, first + 1)
    total, y_flux, link_y, _ = lax.fori_loop(first + 2, last - 1, second, carry, unroll=15)
    part_ref[0:rows] = total
    part_ref[rows : rows + ROWS] = y_flux
    part_ref[rows + ROWS :] = link_y


def start_flow(tx_ref, h_ref, x):
    return tx_ref[x] * h_ref[x]


def edges_kernel(
    storage,
    begin_ref, end_ref, near_ref, corner_ref,
    part_ref, v_in, tx_in, ty_in, tz_in, w_in, ws_in, rr_in, ss_in,
    sums_ref, v_ref, tx_ref, ty_ref, tz_ref, w_ref, ws_ref, rr_ref, ss_ref,
):
    wide, _, depth = v_ref.shape
    planes, rows = wide - 2 * HALO, begin_ref.shape[1]
    walls = Walls(planes, rows, depth)
    first, last = HALO, HALO + planes - 1
    group, row = walls.group, walls.row
    ones = jnp.ones((rows, depth), jnp.float32)
    zeros = jnp.zeros((rows, depth), jnp.float32)
    for d in range(HALO):
        for side, recv, x, there in (
            (1, end_ref, first - 1 - d, group > 0),
            (0, begin_ref, last + 1 + d, group < walls.groups - 1),
        ):
            side_r, side_source, own_source = ones, zeros, zeros
            if d < HALO - 1:
                at = (HALO - 1) * side + d
                near, far = near_ref[planes + at], corner_ref[at]
                side_r, side_source = halo_rows(near, far, walls.core, walls.tile, walls.tiles)
                own_source = recv[4 + d]
            rr_ref[x, 0:rows] = jnp.where(there, recv[d], 1.0)
            rr_ref[x, rows:ROWS] = jnp.where(there, side_r, 1.0)
            ss_ref[x, 0:rows] = jnp.where(there, own_source, 0.0)
            ss_ref[x, rows:ROWS] = jnp.where(there, side_source, 0.0)

    refs = tx_ref, ty_ref, tz_ref, w_ref, ws_ref
    for begin, end in ((1, first), (last, wide - 2)):
        before = tx_ref[last - 1] if begin == last else 2.0 / (rr_ref[0] + rr_ref[1])
        for x in range(begin, end + 1):
            wall = {first - 1: group == 0, last: group == walls.groups - 1}.get(x)
            before = walls.faces(storage, x, before, rr_ref, ss_ref, refs, wall)

    total = part_ref[0:rows]
    y_flux = part_ref[rows : rows + ROWS]
    link_y = part_ref[rows + ROWS :]
    for begin, end in ((2, first + 1), (last - 1, wide - 3)):
        before = start_flow(tx_ref, ws_ref, begin - 1)
        for x in range(begin, end + 1):
            ty = ty_ref[x]
            v, before = relax(
                ws_ref[x], ws_ref[x + 1], before, tx_ref[x], ty, tz_ref[x], w_ref[x], ws_ref[x], depth
            )
            v_ref[x] = v
            if first <= x <= last:
                total = total + ss_ref[x, 0:rows] - storage * v[0:rows]
                y_flux = y_flux + ty * (v - pltpu.roll(v, ROWS - 1, 0))
                link_y = link_y + ty[0:rows]

    out_left = tx_ref[first - 1, 0:rows] * (v_ref[first, 0:rows] - v_ref[first - 1, 0:rows])
    out_right = tx_ref[last, 0:rows] * (v_ref[last, 0:rows] - v_ref[last + 1, 0:rows])
    side = jnp.where(row == ROWS - 1, y_flux, jnp.where(row == rows - 1, -y_flux, 0.0))
    rhs = total - out_left - out_right + side[0:rows] + side[rows:ROWS]
    rhs = jnp.sum(rhs, keepdims=True)
    link_x = jnp.sum(tx_ref[last, 0:rows], keepdims=True)
    link_y = jnp.sum(jnp.where(row[0:rows] == rows - 1, link_y, 0.0), keepdims=True)
    lane = lax.broadcasted_iota(jnp.int32, (1, 128), 1) - (32 * group + 4 * walls.y)
    packed = jnp.where(lane == 0, rhs, 0.0) + jnp.where(lane == 1, link_x, 0.0)
    packed = packed + jnp.where(lane == 2, link_y, 0.0)
    for peer in range(sums_ref.shape[0]):
        sums_ref[peer] = packed


def relax(h, h_next, before, tx, ty, tz, w, ws, depth):
    ahead = tx * h
    flow = before + tx * h_next
    flow = flow + ty * pltpu.roll(h, h.shape[0] - 1, 0) + pltpu.roll(ty * h, 1, 0)
    flow = flow + tz * pltpu.roll(h, depth - 1, 1) + pltpu.roll(tz * h, 1, 1)
    return (1.0 - RELAX) * h + ws + w * flow, ahead


def merge_kernel(part_ref, out_ref):
    total = part_ref[0]
    for peer in range(1, part_ref.shape[0]):
        total = total + part_ref[peer]
    for peer in range(out_ref.shape[0]):
        out_ref[peer] = total


def before_by(pair, stride):
    even, odd = pair
    length = even.shape[0]
    if stride == 1:
        return pltpu.roll(odd, 1, 0), even
    shift = stride // 2
    return pltpu.roll(even, shift, 0), pltpu.roll(odd, shift, 0)


def after_by(pair, stride):
    even, odd = pair
    length = even.shape[0]
    if stride == 1:
        return odd, pltpu.roll(even, length - 1, 0)
    shift = length - stride // 2
    return pltpu.roll(even, shift, 0), pltpu.roll(odd, shift, 0)


def each(fn, *pairs):
    return tuple(fn(*values) for values in zip(*pairs, strict=True))


def coarse_solve(sums_ref, store_brick, levels):
    lines = sums_ref.shape[0] // 2
    lanes = sums_ref.shape[2]
    y_lane = lax.broadcasted_iota(jnp.int32, (8, lanes), 1) // 4 % 8
    own_y = y_lane == lax.broadcasted_iota(jnp.int32, (8, lanes), 0)

    def unpack(line):
        line = jnp.where(own_y, jnp.broadcast_to(line, (8, lanes)), 0.0)
        for shift in (16, 8, 4):
            line = line + pltpu.roll(line, lanes - shift, 1)
        return line

    rhs = tuple(
        jnp.concatenate([unpack(sums_ref[2 * z + core]) for z in range(lines)], axis=0)
        for core in range(2)
    )
    link_x = each(lambda a: pltpu.roll(a, lanes - 1, 1), rhs)
    link_y = each(lambda a: pltpu.roll(a, lanes - 2, 1), rhs)
    link_x_before = each(lambda a: pltpu.roll(a, 32, 1), link_x)
    link_y_before = before_by(link_y, 1)
    diagonal = each(lambda a, b, c, d: store_brick + a + b + c + d, link_x, link_x_before, link_y, link_y_before)
    upper = each(lambda a: -a, link_y)
    alphas, gammas = [], []
    for level in range(levels):
        stride = 1 << level
        inverse = each(lambda d: 1.0 / d, diagonal)
        ratio = each(lambda u, i: -u * i, upper, inverse)
        alpha = before_by(ratio, stride)
        gamma = each(lambda u, i: -u * i, upper, after_by(inverse, stride))
        low = before_by(each(lambda q, u: q * u, ratio, upper), stride)
        diagonal = each(lambda d, a, g, u: d + a + g * u, diagonal, low, gamma, upper)
        upper = each(lambda g, u: g * u, gamma, after_by(upper, stride))
        alphas.append(alpha)
        gammas.append(gamma)
    inverse = each(lambda d: 1.0 / d, diagonal)
    correction = None
    for sweep_no in range(COARSE_ITERS):
        now = rhs
        if sweep_no:
            now = each(
                lambda r, a, b, c: r + a * pltpu.roll(c, 32, 1) + b * pltpu.roll(c, lanes - 32, 1),
                rhs, link_x_before, link_x, correction,
            )
        for level in range(levels):
            stride = 1 << level
            now = each(
                lambda n, a, p, g, q: n + a * p + g * q,
                now, alphas[level], before_by(now, stride), gammas[level], after_by(now, stride),
            )
        correction = each(lambda n, i: n * i, now, inverse)
    return correction


def last_kernel(
    store_brick, levels, chunks,
    sums_ref, v_ref, tx_ref, ty_ref, tz_ref, w_ref, ws_ref,
    out_ref,
    lines_ref, g_ref, done_ref, sems,
):
    group, tile, core, _ = position()
    planes, rows, depth = out_ref.shape
    even, odd = coarse_solve(sums_ref, store_brick, levels)
    length = even.shape[0]
    for parity, line in ((0, even), (1, odd)):
        lines_ref[parity, 0:8] = jnp.zeros((8, line.shape[1]), jnp.float32)
        lines_ref[parity, 8 : 8 + length] = line
        lines_ref[parity, 8 + length : 16 + length] = jnp.zeros((8, line.shape[1]), jnp.float32)
    half = tile // 2
    here = lines_ref[core, pl.ds(8 + half, 1), :]
    ahead = lines_ref[1 - core, pl.ds(8 + half + core, 1), :]
    behind = lines_ref[1 - core, pl.ds(7 + half + core, 1), :]
    lane = lax.broadcasted_iota(jnp.int32, here.shape, 1)
    row = lax.broadcasted_iota(jnp.int32, (ROWS, depth), 0)

    def shift_of(offset):
        own, up, down = (
            jnp.sum(jnp.where(lane == 32 * (group + offset), line, 0.0), keepdims=True)
            for line in (here, ahead, behind)
        )
        return jnp.where(row < rows, own, jnp.where(row < rows + HALO, up, down))

    shifts = [shift_of(offset) for offset in (-1, 0, 1)]
    first, end = HALO, HALO + planes

    def third(x, h, h_next, before):
        v, ahead = relax(h, h_next, before, tx_ref[x], ty_ref[x], tz_ref[x], w_ref[x], ws_ref[x], depth)
        g_ref[x] = v
        return ahead

    def third_inside(x, carry):
        h, before = carry
        h_next = v_ref[x + 1] + shifts[1]
        return h_next, third(x, h, h_next, before)

    h = v_ref[first - 1] + shifts[0]
    h_next = v_ref[first] + shifts[1]
    before = third(first - 1, h, h_next, tx_ref[first - 2] * (v_ref[first - 2] + shifts[0]))
    h, before = lax.fori_loop(first, end - 1, third_inside, (h_next, before), unroll=31)
    h_next = v_ref[end] + shifts[2]
    before = third(end - 1, h, h_next, before)
    third(end, h_next, v_ref[end + 1] + shifts[2], before)

    def fourth(x, before):
        h = g_ref[x]
        h_own = h[0:rows]
        tx = tx_ref[x, 0:rows]
        tz = tz_ref[x, 0:rows]
        ty = ty_ref[x]
        ahead = tx * h_own
        flow = before + tx * g_ref[x + 1, 0:rows]
        flow = flow + (ty * pltpu.roll(h, ROWS - 1, 0) + pltpu.roll(ty * h, 1, 0))[0:rows]
        flow = flow + tz * pltpu.roll(h_own, depth - 1, 1) + pltpu.roll(tz * h_own, 1, 1)
        done_ref[x - HALO] = (1.0 - RELAX) * h_own + ws_ref[x, 0:rows] + w_ref[x, 0:rows] * flow
        return ahead

    before = tx_ref[first - 1, 0:rows] * g_ref[first - 1, 0:rows]
    step = planes // chunks
    copies = []
    for chunk in range(chunks):
        begin = first + chunk * step
        before = lax.fori_loop(begin, begin + step, fourth, before, unroll=16)
        part = pl.ds(chunk * step, step)
        copies.append(pltpu.make_async_copy(done_ref.at[part], out_ref.at[part], sems.at[chunk]))
        copies[-1].start()
    for copy in copies:
        copy.wait()


def spread(block, axes):
    return lax.all_to_all(block, axes, 0, 0)


def on_device(facies, perm_table, source):
    planes, rows, depth = source.shape
    storage = 0.01 / rows
    groups = lax.axis_size("group")
    z_size, y_size, cores = (lax.axis_size(a) for a in TILE_AXES)
    tiles = z_size * y_size * cores
    brick = f32(planes, rows, depth)
    chunks = 4
    r, source, near, far = call(
        functools.partial(rows_kernel, chunks),
        (brick, brick, f32(planes + 2 * (HALO - 1), rows, depth), f32(planes + 4 * HALO, rows, depth)),
        [HBM] * 3,
        [
            pltpu.SMEM(perm_table.shape, jnp.float32),
            pltpu.VMEM(source.shape, jnp.int32),
            pltpu.SemaphoreType.DMA,
            pltpu.SemaphoreType.DMA((2, chunks)),
        ],
        name="rows",
    )(*(pltpu.with_memory_space_constraint(a, pltpu.HBM) for a in (perm_table, facies, source)))
    pairs = [p for i in range(1, tiles - 1, 2) for p in ((i, i + 1), (i + 1, i))]
    far = lax.ppermute(far, TILE_AXES, pairs)
    slab = f32(7, rows, depth)
    begin, end = call(planes_kernel, (slab, slab), [VMEM] * 2, name="planes")(r, source)
    end = lax.ppermute(end, "group", [(i, i + 1) for i in range(groups - 1)])
    begin = lax.ppermute(begin, "group", [(i + 1, i) for i in range(groups - 1)])
    near, corner = call(
        corners_kernel,
        (f32(*near.shape), f32(2 * (HALO - 1), rows, depth)),
        [VMEM] * 3,
        name="corners",
        aliases={2: 0},
    )(begin, end, near)
    near = lax.ppermute(near, "core", [(0, 1), (1, 0)])
    corner = lax.ppermute(corner, TILE_AXES, pairs)
    wide = f32(planes + 2 * HALO, ROWS, depth)
    part, *fields = call(
        functools.partial(middle_kernel, storage),
        (f32(2 * rows + ROWS, depth),) + (wide,) * 8,
        [VMEM] * 4,
        name="middle",
    )(r, source, near, far)
    sums, *fields = call(
        functools.partial(edges_kernel, storage),
        (f32(groups * y_size, 1, 128),) + (wide,) * 8,
        [VMEM] * 13,
        name="edges",
        aliases={5 + i: 1 + i for i in range(8)},
    )(begin, end, near, corner, part, *fields)
    fields = fields[:6]
    sums = spread(sums, ("group", "y"))
    sums = call(merge_kernel, f32(z_size * cores, 1, 128), [VMEM], name="merge")(sums)
    sums = spread(sums, ("z", "core"))
    length = z_size * y_size
    chunks = 4
    return call(
        functools.partial(last_kernel, storage * planes * rows * depth, tiles.bit_length() - 1, chunks),
        brick,
        [VMEM] * 7,
        [
            pltpu.VMEM((2, length + 16, 128), jnp.float32),
            pltpu.VMEM(wide.shape, jnp.float32),
            pltpu.VMEM(brick.shape, jnp.float32),
            pltpu.SemaphoreType.DMA((chunks,)),
        ],
        name="last",
        out_spec=HBM,
    )(sums, *fields)


def solution(mesh):
    groups, tiles = mesh.shape["group"], mesh.shape["tile"]
    chips = Mesh(mesh.devices.reshape(groups, tiles // 16, 8, 2), ("group",) + TILE_AXES)
    cells = P("group", TILE_AXES, None)
    return jax.shard_map(
        on_device, mesh=chips, in_specs=(cells, P(), cells), out_specs=cells, check_vma=False
    )
```

```python
import functools

import jax
import jax.numpy as jnp
from jax import lax
from jax.experimental import pallas as pl
from jax.experimental.pallas import tpu as pltpu
from jax.sharding import Mesh
from jax.sharding import PartitionSpec as P

COARSE_ITERS = 3
RELAX = 0.8
HALO = 4
TILE_AXES = ("z", "y", "core")
ROWS = 16
VMEM = pl.BlockSpec(memory_space=pltpu.VMEM)
HBM = pl.BlockSpec(memory_space=pltpu.HBM)


def position():
    z, y, core = (lax.axis_index(a) for a in TILE_AXES)
    tile = (z * lax.axis_size("y") + y) * lax.axis_size("core") + core
    return lax.axis_index("group"), tile, core, y


def call(kernel, out_shape, in_specs, scratch=(), name=None, aliases=None, out_spec=VMEM):
    outs = jax.tree.map(lambda _: out_spec, out_shape)
    return pl.pallas_call(
        kernel,
        out_shape=out_shape,
        in_specs=in_specs,
        out_specs=outs,
        scratch_shapes=list(scratch),
        name=name,
        input_output_aliases=aliases or {},
        compiler_params=pltpu.CompilerParams(vmem_limit_bytes=24 * 1024 * 1024),
    )


def f32(*shape):
    return jax.ShapeDtypeStruct(shape, jnp.float32)


def low_half(shape):
    return lax.broadcasted_iota(jnp.int32, shape, 0) < shape[0] // 2


def row_tiles(r, source):
    low = low_half(r.shape)
    half = r.shape[0] // 2
    return jnp.where(low, r, pltpu.roll(source, half, 0)), jnp.where(low, pltpu.roll(r, half, 0), source)


def rows_kernel(
    chunks, table_hbm, facies_hbm, source_hbm, r_ref, source_ref, near_ref, far_ref,
    table_ref, facies_ref, table_sem, sems,
):
    core = position()[2]
    planes, rows, depth = facies_ref.shape
    kinds = table_ref.shape[0]
    first = core == 0
    step = planes // chunks
    table = pltpu.make_async_copy(table_hbm, table_ref, table_sem)
    table.start()
    copies = []
    for chunk in range(chunks):
        part = pl.ds(chunk * step, step)
        pair = (
            pltpu.make_async_copy(facies_hbm.at[part], facies_ref.at[part], sems.at[0, chunk]),
            pltpu.make_async_copy(source_hbm.at[part], source_ref.at[part], sems.at[1, chunk]),
        )
        for copy in pair:
            copy.start()
        copies.append(pair)
    table.wait()

    for chunk in range(chunks):
        for copy in copies[chunk]:
            copy.wait()

        def body(x, carry):
            facies = facies_ref[x]
            perm = jnp.full((rows, depth), table_ref[0], jnp.float32)
            for kind in range(1, kinds):
                perm = jnp.where(facies == kind, table_ref[kind], perm)
            r = 1.0 / perm
            source = source_ref[x]
            r_ref[x] = r
            begin, end = row_tiles(r, source)
            near_ref[x] = jnp.where(first, end, begin)
            far_ref[x] = jnp.where(first, begin, end)
            return carry

        lax.fori_loop(chunk * step, (chunk + 1) * step, body, 0, unroll=8)
    for x in range(planes, far_ref.shape[0]):
        far_ref[x] = jnp.zeros((rows, depth), jnp.float32)


def halo_rows(near, far, core, tile, tiles):
    low = low_half(near.shape)
    first = core == 0
    after = jnp.where(first, near, far)
    before = jnp.where(first, far, near)
    half = near.shape[0] // 2
    r = jnp.where(low, after, pltpu.roll(before, half, 0))
    source = jnp.where(low, pltpu.roll(after, half, 0), before)
    absent = (low & (tile == tiles - 1)) | (~low & (tile == 0))
    return jnp.where(absent, 1.0, r), jnp.where(absent, 0.0, source)


def even_group():
    return lax.rem(position()[0], 2) == 0


def planes_kernel(r_ref, source_ref, one_ref, two_ref):
    planes = r_ref.shape[0]
    even = even_group()

    def put(at, field_ref, d):
        begin, end = field_ref[d], field_ref[planes - 1 - d]
        one_ref[at] = jnp.where(even, end, begin)
        two_ref[at] = jnp.where(even, begin, end)

    for d in range(HALO):
        put(d, r_ref, d)
        if d < HALO - 1:
            put(4 + d, source_ref, d)


def came(one_ref, two_ref):
    even = even_group()
    return (
        lambda at: jnp.where(even, one_ref[at], two_ref[at]),
        lambda at: jnp.where(even, two_ref[at], one_ref[at]),
    )


def corners_kernel(one_ref, two_ref, near_in, near_ref, corner_ref):
    first = position()[2] == 0
    count = HALO - 1
    own = near_ref.shape[0] - 2 * count
    for side, recv in enumerate(came(one_ref, two_ref)):
        for d in range(count):
            begin, end = row_tiles(recv(d), recv(4 + d))
            near_ref[own + count * side + d] = jnp.where(first, end, begin)
            corner_ref[count * side + d] = jnp.where(first, begin, end)


class Walls:
    def __init__(self, planes, rows, depth):
        self.group, self.tile, self.core, self.y = position()
        self.groups = lax.axis_size("group")
        self.tiles = lax.axis_size("z") * lax.axis_size("y") * lax.axis_size("core")
        self.planes, self.rows, self.depth = planes, rows, depth
        self.row = lax.broadcasted_iota(jnp.int32, (ROWS, depth), 0)
        column = lax.broadcasted_iota(jnp.int32, (ROWS, depth), 1)
        top = (self.row == ROWS - 1) & (self.tile == 0)
        self.in_y = top | ((self.row == rows - 1) & (self.tile == self.tiles - 1))
        self.in_z = column == depth - 1

    def faces(self, storage, x, before, rr_ref, ss_ref, refs, x_wall=None):
        tx_ref, ty_ref, tz_ref, w_ref, ws_ref = refs
        r = rr_ref[x]
        over_x = r + rr_ref[x + 1]
        over_y = r + pltpu.roll(r, ROWS - 1, 0)
        over_z = r + pltpu.roll(r, self.depth - 1, 1)
        over_xy = over_x * over_y
        share = 2.0 / (over_xy * over_z)
        rest = share * over_z
        tx = rest * over_y
        if x_wall is not None:
            tx = jnp.where(x_wall, 0.0, tx)
        ty = jnp.where(self.in_y, 0.0, rest * over_x)
        tz = jnp.where(self.in_z, 0.0, share * over_xy)
        diagonal = storage + tx + before + ty + pltpu.roll(ty, 1, 0) + tz + pltpu.roll(tz, 1, 1)
        w = RELAX / diagonal
        tx_ref[x] = tx
        ty_ref[x] = ty
        tz_ref[x] = tz
        w_ref[x] = w
        ws_ref[x] = w * ss_ref[x]
        return tx


def middle_kernel(
    storage,
    r_ref, source_ref, near_ref, far_ref,
    part_ref, v_ref, tx_ref, ty_ref, tz_ref, w_ref, ws_ref, rr_ref, ss_ref,
):
    planes, rows, depth = r_ref.shape
    walls = Walls(planes, rows, depth)
    first, last = HALO, HALO + planes - 1

    def gather_rows(x, carry):
        side_r, side_source = halo_rows(near_ref[x], far_ref[x], walls.core, walls.tile, walls.tiles)
        rr_ref[HALO + x, 0:rows] = r_ref[x]
        rr_ref[HALO + x, rows:ROWS] = side_r
        ss_ref[HALO + x, 0:rows] = source_ref[x]
        ss_ref[HALO + x, rows:ROWS] = side_source
        return carry

    lax.fori_loop(0, planes, gather_rows, 0, unroll=16)
    refs = tx_ref, ty_ref, tz_ref, w_ref, ws_ref

    def faces(x, before):
        return walls.faces(storage, x, before, rr_ref, ss_ref, refs)

    start = 2.0 / (rr_ref[first] + rr_ref[first + 1])
    tx_ref[first] = start
    lax.fori_loop(first + 1, last, faces, start, unroll=31)

    def second(x, carry):
        total, y_flux, link_y, before = carry
        ty = ty_ref[x]
        v, ahead = relax(
            ws_ref[x], ws_ref[x + 1], before, tx_ref[x], ty, tz_ref[x], w_ref[x], ws_ref[x], depth
        )
        v_ref[x] = v
        total = total + ss_ref[x, 0:rows] - storage * v[0:rows]
        y_flux = y_flux + ty * (v - pltpu.roll(v, ROWS - 1, 0))
        return total, y_flux, link_y + ty[0:rows], ahead

    zeros = jnp.zeros((rows, depth), jnp.float32)
    carry = zeros, jnp.zeros((ROWS, depth), jnp.float32), zeros, start_flow(tx_ref, ws_ref, first + 1)
    total, y_flux, link_y, _ = lax.fori_loop(first + 2, last - 1, second, carry, unroll=15)
    part_ref[0:rows] = total
    part_ref[rows : rows + ROWS] = y_flux
    part_ref[rows + ROWS :] = link_y


def start_flow(tx_ref, h_ref, x):
    return tx_ref[x] * h_ref[x]


def edges_kernel(
    storage,
    one_ref, two_ref, near_ref, corner_ref,
    part_ref, v_in, tx_in, ty_in, tz_in, w_in, ws_in, rr_in, ss_in,
    sums_ref, v_ref, tx_ref, ty_ref, tz_ref, w_ref, ws_ref, rr_ref, ss_ref,
):
    wide, _, depth = v_ref.shape
    planes, rows = wide - 2 * HALO, one_ref.shape[1]
    walls = Walls(planes, rows, depth)
    first, last = HALO, HALO + planes - 1
    group, row = walls.group, walls.row
    ones = jnp.ones((rows, depth), jnp.float32)
    zeros = jnp.zeros((rows, depth), jnp.float32)
    following, preceding = came(one_ref, two_ref)
    for d in range(HALO):
        for side, recv, x, there in (
            (1, preceding, first - 1 - d, group > 0),
            (0, following, last + 1 + d, group < walls.groups - 1),
        ):
            side_r, side_source, own_source = ones, zeros, zeros
            if d < HALO - 1:
                at = (HALO - 1) * side + d
                near, far = near_ref[planes + at], corner_ref[at]
                side_r, side_source = halo_rows(near, far, walls.core, walls.tile, walls.tiles)
                own_source = recv(4 + d)
            rr_ref[x, 0:rows] = jnp.where(there, recv(d), 1.0)
            rr_ref[x, rows:ROWS] = jnp.where(there, side_r, 1.0)
            ss_ref[x, 0:rows] = jnp.where(there, own_source, 0.0)
            ss_ref[x, rows:ROWS] = jnp.where(there, side_source, 0.0)

    refs = tx_ref, ty_ref, tz_ref, w_ref, ws_ref
    for begin, end in ((1, first), (last, wide - 2)):
        before = tx_ref[last - 1] if begin == last else 2.0 / (rr_ref[0] + rr_ref[1])
        for x in range(begin, end + 1):
            wall = {first - 1: group == 0, last: group == walls.groups - 1}.get(x)
            before = walls.faces(storage, x, before, rr_ref, ss_ref, refs, wall)

    total = part_ref[0:rows]
    y_flux = part_ref[rows : rows + ROWS]
    link_y = part_ref[rows + ROWS :]
    for begin, end in ((2, first + 1), (last - 1, wide - 3)):
        before = start_flow(tx_ref, ws_ref, begin - 1)
        for x in range(begin, end + 1):
            ty = ty_ref[x]
            v, before = relax(
                ws_ref[x], ws_ref[x + 1], before, tx_ref[x], ty, tz_ref[x], w_ref[x], ws_ref[x], depth
            )
            v_ref[x] = v
            if first <= x <= last:
                total = total + ss_ref[x, 0:rows] - storage * v[0:rows]
                y_flux = y_flux + ty * (v - pltpu.roll(v, ROWS - 1, 0))
                link_y = link_y + ty[0:rows]

    out_left = tx_ref[first - 1, 0:rows] * (v_ref[first, 0:rows] - v_ref[first - 1, 0:rows])
    out_right = tx_ref[last, 0:rows] * (v_ref[last, 0:rows] - v_ref[last + 1, 0:rows])
    side = jnp.where(row == ROWS - 1, y_flux, jnp.where(row == rows - 1, -y_flux, 0.0))
    rhs = total - out_left - out_right + side[0:rows] + side[rows:ROWS]
    rhs = jnp.sum(rhs, keepdims=True)
    link_x = jnp.sum(tx_ref[last, 0:rows], keepdims=True)
    link_y = jnp.sum(jnp.where(row[0:rows] == rows - 1, link_y, 0.0), keepdims=True)
    lane = lax.broadcasted_iota(jnp.int32, (1, 128), 1) - (32 * group + 4 * walls.y)
    packed = jnp.where(lane == 0, rhs, 0.0) + jnp.where(lane == 1, link_x, 0.0)
    packed = packed + jnp.where(lane == 2, link_y, 0.0)
    for peer in range(sums_ref.shape[0]):
        sums_ref[peer] = packed


def relax(h, h_next, before, tx, ty, tz, w, ws, depth):
    ahead = tx * h
    flow = before + tx * h_next
    flow = flow + ty * pltpu.roll(h, h.shape[0] - 1, 0) + pltpu.roll(ty * h, 1, 0)
    flow = flow + tz * pltpu.roll(h, depth - 1, 1) + pltpu.roll(tz * h, 1, 1)
    return (1.0 - RELAX) * h + ws + w * flow, ahead


def merge_kernel(part_ref, out_ref):
    total = part_ref[0]
    for peer in range(1, part_ref.shape[0]):
        total = total + part_ref[peer]
    for peer in range(out_ref.shape[0]):
        out_ref[peer] = total


def before_by(pair, stride):
    even, odd = pair
    length = even.shape[0]
    if stride == 1:
        return pltpu.roll(odd, 1, 0), even
    shift = stride // 2
    return pltpu.roll(even, shift, 0), pltpu.roll(odd, shift, 0)


def after_by(pair, stride):
    even, odd = pair
    length = even.shape[0]
    if stride == 1:
        return odd, pltpu.roll(even, length - 1, 0)
    shift = length - stride // 2
    return pltpu.roll(even, shift, 0), pltpu.roll(odd, shift, 0)


def each(fn, *pairs):
    return tuple(fn(*values) for values in zip(*pairs, strict=True))


def coarse_solve(sums_ref, store_brick, levels):
    lines = sums_ref.shape[0] // 2
    lanes = sums_ref.shape[2]
    y_lane = lax.broadcasted_iota(jnp.int32, (8, lanes), 1) // 4 % 8
    own_y = y_lane == lax.broadcasted_iota(jnp.int32, (8, lanes), 0)

    def unpack(line):
        line = jnp.where(own_y, jnp.broadcast_to(line, (8, lanes)), 0.0)
        for shift in (16, 8, 4):
            line = line + pltpu.roll(line, lanes - shift, 1)
        return line

    rhs = tuple(
        jnp.concatenate([unpack(sums_ref[2 * z + core]) for z in range(lines)], axis=0)
        for core in range(2)
    )
    link_x = each(lambda a: pltpu.roll(a, lanes - 1, 1), rhs)
    link_y = each(lambda a: pltpu.roll(a, lanes - 2, 1), rhs)
    link_x_before = each(lambda a: pltpu.roll(a, 32, 1), link_x)
    link_y_before = before_by(link_y, 1)
    diagonal = each(lambda a, b, c, d: store_brick + a + b + c + d, link_x, link_x_before, link_y, link_y_before)
    upper = each(lambda a: -a, link_y)
    alphas, gammas = [], []
    for level in range(levels):
        stride = 1 << level
        inverse = each(lambda d: 1.0 / d, diagonal)
        ratio = each(lambda u, i: -u * i, upper, inverse)
        alpha = before_by(ratio, stride)
        gamma = each(lambda u, i: -u * i, upper, after_by(inverse, stride))
        low = before_by(each(lambda q, u: q * u, ratio, upper), stride)
        diagonal = each(lambda d, a, g, u: d + a + g * u, diagonal, low, gamma, upper)
        upper = each(lambda g, u: g * u, gamma, after_by(upper, stride))
        alphas.append(alpha)
        gammas.append(gamma)
    inverse = each(lambda d: 1.0 / d, diagonal)
    correction = None
    for sweep_no in range(COARSE_ITERS):
        now = rhs
        if sweep_no:
            now = each(
                lambda r, a, b, c: r + a * pltpu.roll(c, 32, 1) + b * pltpu.roll(c, lanes - 32, 1),
                rhs, link_x_before, link_x, correction,
            )
        for level in range(levels):
            stride = 1 << level
            now = each(
                lambda n, a, p, g, q: n + a * p + g * q,
                now, alphas[level], before_by(now, stride), gammas[level], after_by(now, stride),
            )
        correction = each(lambda n, i: n * i, now, inverse)
    return correction


def last_kernel(
    store_brick, levels, chunks,
    sums_ref, v_ref, tx_ref, ty_ref, tz_ref, w_ref, ws_ref,
    out_ref,
    lines_ref, g_ref, done_ref, sems,
):
    group, tile, core, _ = position()
    planes, rows, depth = out_ref.shape
    even, odd = coarse_solve(sums_ref, store_brick, levels)
    length = even.shape[0]
    for parity, line in ((0, even), (1, odd)):
        lines_ref[parity, 0:8] = jnp.zeros((8, line.shape[1]), jnp.float32)
        lines_ref[parity, 8 : 8 + length] = line
        lines_ref[parity, 8 + length : 16 + length] = jnp.zeros((8, line.shape[1]), jnp.float32)
    half = tile // 2
    here = lines_ref[core, pl.ds(8 + half, 1), :]
    ahead = lines_ref[1 - core, pl.ds(8 + half + core, 1), :]
    behind = lines_ref[1 - core, pl.ds(7 + half + core, 1), :]
    lane = lax.broadcasted_iota(jnp.int32, here.shape, 1)
    row = lax.broadcasted_iota(jnp.int32, (ROWS, depth), 0)

    def shift_of(offset):
        own, up, down = (
            jnp.sum(jnp.where(lane == 32 * (group + offset), line, 0.0), keepdims=True)
            for line in (here, ahead, behind)
        )
        return jnp.where(row < rows, own, jnp.where(row < rows + HALO, up, down))

    shifts = [shift_of(offset) for offset in (-1, 0, 1)]
    first, end = HALO, HALO + planes

    def third(x, h, h_next, before):
        v, ahead = relax(h, h_next, before, tx_ref[x], ty_ref[x], tz_ref[x], w_ref[x], ws_ref[x], depth)
        g_ref[x] = v
        return ahead

    def third_inside(x, carry):
        h, before = carry
        h_next = v_ref[x + 1] + shifts[1]
        return h_next, third(x, h, h_next, before)

    h = v_ref[first - 1] + shifts[0]
    h_next = v_ref[first] + shifts[1]
    before = third(first - 1, h, h_next, tx_ref[first - 2] * (v_ref[first - 2] + shifts[0]))
    h, before = lax.fori_loop(first, end - 1, third_inside, (h_next, before), unroll=31)
    h_next = v_ref[end] + shifts[2]
    before = third(end - 1, h, h_next, before)
    third(end, h_next, v_ref[end + 1] + shifts[2], before)

    def fourth(x, before):
        h = g_ref[x]
        h_own = h[0:rows]
        tx = tx_ref[x, 0:rows]
        tz = tz_ref[x, 0:rows]
        ty = ty_ref[x]
        ahead = tx * h_own
        flow = before + tx * g_ref[x + 1, 0:rows]
        flow = flow + (ty * pltpu.roll(h, ROWS - 1, 0) + pltpu.roll(ty * h, 1, 0))[0:rows]
        flow = flow + tz * pltpu.roll(h_own, depth - 1, 1) + pltpu.roll(tz * h_own, 1, 1)
        done_ref[x - HALO] = (1.0 - RELAX) * h_own + ws_ref[x, 0:rows] + w_ref[x, 0:rows] * flow
        return ahead

    before = tx_ref[first - 1, 0:rows] * g_ref[first - 1, 0:rows]
    step = planes // chunks
    copies = []
    for chunk in range(chunks):
        begin = first + chunk * step
        before = lax.fori_loop(begin, begin + step, fourth, before, unroll=16)
        part = pl.ds(chunk * step, step)
        copies.append(pltpu.make_async_copy(done_ref.at[part], out_ref.at[part], sems.at[chunk]))
        copies[-1].start()
    for copy in copies:
        copy.wait()


def spread(block, axes):
    return lax.all_to_all(block, axes, 0, 0)


def on_device(facies, perm_table, source):
    planes, rows, depth = source.shape
    storage = 0.01 / rows
    groups = lax.axis_size("group")
    z_size, y_size, cores = (lax.axis_size(a) for a in TILE_AXES)
    tiles = z_size * y_size * cores
    brick = f32(planes, rows, depth)
    chunks = 4
    r, source, near, far = call(
        functools.partial(rows_kernel, chunks),
        (brick, brick, f32(planes + 2 * (HALO - 1), rows, depth), f32(planes + 4 * HALO, rows, depth)),
        [HBM] * 3,
        [
            pltpu.SMEM(perm_table.shape, jnp.float32),
            pltpu.VMEM(source.shape, jnp.int32),
            pltpu.SemaphoreType.DMA,
            pltpu.SemaphoreType.DMA((2, chunks)),
        ],
        name="rows",
    )(*(pltpu.with_memory_space_constraint(a, pltpu.HBM) for a in (perm_table, facies, source)))
    pairs = [p for i in range(1, tiles - 1, 2) for p in ((i, i + 1), (i + 1, i))]
    far = lax.ppermute(far, TILE_AXES, pairs)
    slab = f32(7, rows, depth)
    one, two = call(planes_kernel, (slab, slab), [VMEM] * 2, name="planes")(r, source)
    one, two = (
        lax.ppermute(a, "group", [p for i in range(b, groups - 1, 2) for p in ((i, i + 1), (i + 1, i))])
        for a, b in ((one, 0), (two, 1))
    )
    near, corner = call(
        corners_kernel,
        (f32(*near.shape), f32(2 * (HALO - 1), rows, depth)),
        [VMEM] * 3,
        name="corners",
        aliases={2: 0},
    )(one, two, near)
    near = lax.ppermute(near, "core", [(0, 1), (1, 0)])
    corner = lax.ppermute(corner, TILE_AXES, pairs)
    wide = f32(planes + 2 * HALO, ROWS, depth)
    part, *fields = call(
        functools.partial(middle_kernel, storage),
        (f32(2 * rows + ROWS, depth),) + (wide,) * 8,
        [VMEM] * 4,
        name="middle",
    )(r, source, near, far)
    sums, *fields = call(
        functools.partial(edges_kernel, storage),
        (f32(groups * y_size, 1, 128),) + (wide,) * 8,
        [VMEM] * 13,
        name="edges",
        aliases={5 + i: 1 + i for i in range(8)},
    )(one, two, near, corner, part, *fields)
    fields = fields[:6]
    sums = spread(sums, ("group", "y"))
    sums = call(merge_kernel, f32(z_size * cores, 1, 128), [VMEM], name="merge")(sums)
    sums = spread(sums, ("z", "core"))
    length = z_size * y_size
    chunks = 4
    return call(
        functools.partial(last_kernel, storage * planes * rows * depth, tiles.bit_length() - 1, chunks),
        brick,
        [VMEM] * 7,
        [
            pltpu.VMEM((2, length + 16, 128), jnp.float32),
            pltpu.VMEM(wide.shape, jnp.float32),
            pltpu.VMEM(brick.shape, jnp.float32),
            pltpu.SemaphoreType.DMA((chunks,)),
        ],
        name="last",
        out_spec=HBM,
    )(sums, *fields)


def solution(mesh):
    groups, tiles = mesh.shape["group"], mesh.shape["tile"]
    chips = Mesh(mesh.devices.reshape(groups, tiles // 16, 8, 2), ("group",) + TILE_AXES)
    cells = P("group", TILE_AXES, None)
    return jax.shard_map(
        on_device, mesh=chips, in_specs=(cells, P(), cells), out_specs=cells, check_vma=False
    )
```

```python
import functools

import jax
import jax.numpy as jnp
from jax import lax
from jax.experimental import pallas as pl
from jax.experimental.pallas import tpu as pltpu
from jax.sharding import Mesh
from jax.sharding import PartitionSpec as P

COARSE_ITERS = 3
RELAX = 0.8
HALO = 4
TILE_AXES = ("z", "y", "core")
ROWS = 16
VMEM = pl.BlockSpec(memory_space=pltpu.VMEM)
HBM = pl.BlockSpec(memory_space=pltpu.HBM)


def position():
    z, y, core = (lax.axis_index(a) for a in TILE_AXES)
    tile = (z * lax.axis_size("y") + y) * lax.axis_size("core") + core
    return lax.axis_index("group"), tile, core, y


def call(kernel, out_shape, in_specs, scratch=(), name=None, aliases=None, out_spec=VMEM):
    outs = jax.tree.map(lambda _: out_spec, out_shape)
    return pl.pallas_call(
        kernel,
        out_shape=out_shape,
        in_specs=in_specs,
        out_specs=outs,
        scratch_shapes=list(scratch),
        name=name,
        input_output_aliases=aliases or {},
        compiler_params=pltpu.CompilerParams(vmem_limit_bytes=24 * 1024 * 1024),
    )


def f32(*shape):
    return jax.ShapeDtypeStruct(shape, jnp.float32)


def low_half(shape):
    return lax.broadcasted_iota(jnp.int32, shape, 0) < shape[0] // 2


def row_tiles(r, source):
    low = low_half(r.shape)
    half = r.shape[0] // 2
    return jnp.where(low, r, pltpu.roll(source, half, 0)), jnp.where(low, pltpu.roll(r, half, 0), source)


def rows_kernel(
    chunks, table_hbm, facies_hbm, source_hbm, r_ref, source_ref, near_ref, far_ref,
    table_ref, facies_ref, table_sem, sems,
):
    core = position()[2]
    planes, rows, depth = facies_ref.shape
    kinds = table_ref.shape[0]
    first = core == 0
    step = planes // chunks
    table = pltpu.make_async_copy(table_hbm, table_ref, table_sem)
    table.start()
    copies = []
    for chunk in range(chunks):
        part = pl.ds(chunk * step, step)
        pair = (
            pltpu.make_async_copy(facies_hbm.at[part], facies_ref.at[part], sems.at[0, chunk]),
            pltpu.make_async_copy(source_hbm.at[part], source_ref.at[part], sems.at[1, chunk]),
        )
        for copy in pair:
            copy.start()
        copies.append(pair)
    table.wait()

    for chunk in range(chunks):
        for copy in copies[chunk]:
            copy.wait()

        def body(x, carry):
            facies = facies_ref[x]
            perm = jnp.full((rows, depth), table_ref[0], jnp.float32)
            for kind in range(1, kinds):
                perm = jnp.where(facies == kind, table_ref[kind], perm)
            r = 1.0 / perm
            source = source_ref[x]
            r_ref[x] = r
            begin, end = row_tiles(r, source)
            near_ref[x] = jnp.where(first, end, begin)
            far_ref[x] = jnp.where(first, begin, end)
            return carry

        lax.fori_loop(chunk * step, (chunk + 1) * step, body, 0, unroll=8)
    for x in range(planes, far_ref.shape[0]):
        far_ref[x] = jnp.zeros((rows, depth), jnp.float32)


def halo_rows(near, far, core, tile, tiles):
    low = low_half(near.shape)
    first = core == 0
    after = jnp.where(first, near, far)
    before = jnp.where(first, far, near)
    half = near.shape[0] // 2
    r = jnp.where(low, after, pltpu.roll(before, half, 0))
    source = jnp.where(low, pltpu.roll(after, half, 0), before)
    absent = (low & (tile == tiles - 1)) | (~low & (tile == 0))
    return jnp.where(absent, 1.0, r), jnp.where(absent, 0.0, source)


def planes_kernel(r_ref, source_ref, begin_ref, end_ref):
    planes = r_ref.shape[0]
    for d in range(HALO):
        for out, x in ((begin_ref, d), (end_ref, planes - 1 - d)):
            out[d] = r_ref[x]
            if d < HALO - 1:
                out[4 + d] = source_ref[x]


def corners_kernel(begin_ref, end_ref, near_in, near_ref, corner_ref):
    first = position()[2] == 0
    count = HALO - 1
    own = near_ref.shape[0] - 2 * count
    for side, recv in enumerate((begin_ref, end_ref)):
        for d in range(count):
            begin, end = row_tiles(recv[d], recv[4 + d])
            near_ref[own + count * side + d] = jnp.where(first, end, begin)
            corner_ref[count * side + d] = jnp.where(first, begin, end)


class Walls:
    def __init__(self, planes, rows, depth):
        self.group, self.tile, self.core, self.y = position()
        self.groups = lax.axis_size("group")
        self.tiles = lax.axis_size("z") * lax.axis_size("y") * lax.axis_size("core")
        self.planes, self.rows, self.depth = planes, rows, depth
        self.row = lax.broadcasted_iota(jnp.int32, (ROWS, depth), 0)
        column = lax.broadcasted_iota(jnp.int32, (ROWS, depth), 1)
        top = (self.row == ROWS - 1) & (self.tile == 0)
        self.in_y = top | ((self.row == rows - 1) & (self.tile == self.tiles - 1))
        self.in_z = column == depth - 1

    def faces(self, storage, x, before, rr_ref, ss_ref, refs, x_wall=None):
        tx_ref, ty_ref, tz_ref, w_ref, ws_ref = refs
        r = rr_ref[x]
        over_x = r + rr_ref[x + 1]
        over_y = r + pltpu.roll(r, ROWS - 1, 0)
        over_z = r + pltpu.roll(r, self.depth - 1, 1)
        over_xy = over_x * over_y
        share = 2.0 / (over_xy * over_z)
        rest = share * over_z
        tx = rest * over_y
        if x_wall is not None:
            tx = jnp.where(x_wall, 0.0, tx)
        ty = jnp.where(self.in_y, 0.0, rest * over_x)
        tz = jnp.where(self.in_z, 0.0, share * over_xy)
        diagonal = storage + tx + before + ty + pltpu.roll(ty, 1, 0) + tz + pltpu.roll(tz, 1, 1)
        w = RELAX / diagonal
        tx_ref[x] = tx
        ty_ref[x] = ty
        tz_ref[x] = tz
        w_ref[x] = w
        ws_ref[x] = w * ss_ref[x]
        return tx


def own_kernel(storage, r_ref, tx_ref, tz_ref, w_ref):
    planes, rows, depth = r_ref.shape
    wall = lax.broadcasted_iota(jnp.int32, (rows, depth), 1) == depth - 1

    def faces(x, before):
        r = r_ref[x]
        over_x = r + r_ref[x + 1]
        over_z = r + pltpu.roll(r, depth - 1, 1)
        share = 2.0 / (over_x * over_z)
        tx = share * over_z
        tz = jnp.where(wall, 0.0, share * over_x)
        tx_ref[HALO + x, 0:rows] = tx
        tz_ref[HALO + x, 0:rows] = tz
        w_ref[HALO + x, 0:rows] = storage + tx + before + tz + pltpu.roll(tz, 1, 1)
        return tx

    start = 2.0 / (r_ref[0] + r_ref[1])
    tx_ref[HALO, 0:rows] = start
    lax.fori_loop(1, planes - 1, faces, start, unroll=31)


def middle_kernel(
    storage,
    r_ref, source_ref, near_ref, far_ref, tx_in, tz_in, w_in,
    part_ref, v_ref, tx_ref, ty_ref, tz_ref, w_ref, ws_ref, rr_ref, ss_ref,
):
    planes, rows, depth = r_ref.shape
    walls = Walls(planes, rows, depth)
    first, last = HALO, HALO + planes - 1

    def gather_rows(x, carry):
        side_r, side_source = halo_rows(near_ref[x], far_ref[x], walls.core, walls.tile, walls.tiles)
        rr_ref[HALO + x, 0:rows] = r_ref[x]
        rr_ref[HALO + x, rows:ROWS] = side_r
        ss_ref[HALO + x, 0:rows] = source_ref[x]
        ss_ref[HALO + x, rows:ROWS] = side_source
        return carry

    lax.fori_loop(0, planes, gather_rows, 0, unroll=16)
    own, beside = pl.ds(0, rows), pl.ds(rows, ROWS - rows)
    in_z = walls.in_z[rows:ROWS]

    def faces(x, before):
        r = rr_ref[x]
        over_y = r + pltpu.roll(r, ROWS - 1, 0)
        r_side = r[rows:ROWS]
        over_x = r_side + rr_ref[x + 1, beside]
        over_z = r_side + pltpu.roll(r_side, depth - 1, 1)
        over_xz = over_x * over_z
        share = 2.0 / (over_xz * over_y[rows:ROWS])
        rest = share * over_y[rows:ROWS]
        tx = rest * over_z
        tz = jnp.where(in_z, 0.0, rest * over_x)
        ty = jnp.concatenate([2.0 / over_y[0:rows], share * over_xz], axis=0)
        ty = jnp.where(walls.in_y, 0.0, ty)
        side = storage + tx + before + tz + pltpu.roll(tz, 1, 1)
        w = RELAX / (jnp.concatenate([w_in[x, own], side], axis=0) + ty + pltpu.roll(ty, 1, 0))
        tx_ref[x, beside] = tx
        ty_ref[x] = ty
        tz_ref[x, beside] = tz
        w_ref[x] = w
        ws_ref[x] = w * ss_ref[x]
        return tx

    start = 2.0 / (rr_ref[first, beside] + rr_ref[first + 1, beside])
    tx_ref[first, beside] = start
    lax.fori_loop(first + 1, last, faces, start, unroll=31)

    def second(x, carry):
        total, y_flux, link_y, before = carry
        ty = ty_ref[x]
        v, ahead = relax(
            ws_ref[x], ws_ref[x + 1], before, tx_ref[x], ty, tz_ref[x], w_ref[x], ws_ref[x], depth
        )
        v_ref[x] = v
        total = total + ss_ref[x, 0:rows] - storage * v[0:rows]
        y_flux = y_flux + ty * (v - pltpu.roll(v, ROWS - 1, 0))
        return total, y_flux, link_y + ty[0:rows], ahead

    zeros = jnp.zeros((rows, depth), jnp.float32)
    carry = zeros, jnp.zeros((ROWS, depth), jnp.float32), zeros, start_flow(tx_ref, ws_ref, first + 1)
    total, y_flux, link_y, _ = lax.fori_loop(first + 2, last - 1, second, carry, unroll=15)
    part_ref[0:rows] = total
    part_ref[rows : rows + ROWS] = y_flux
    part_ref[rows + ROWS :] = link_y


def start_flow(tx_ref, h_ref, x):
    return tx_ref[x] * h_ref[x]


def edges_kernel(
    storage,
    begin_ref, end_ref, near_ref, corner_ref,
    part_ref, v_in, tx_in, ty_in, tz_in, w_in, ws_in, rr_in, ss_in,
    sums_ref, v_ref, tx_ref, ty_ref, tz_ref, w_ref, ws_ref, rr_ref, ss_ref,
):
    wide, _, depth = v_ref.shape
    planes, rows = wide - 2 * HALO, begin_ref.shape[1]
    walls = Walls(planes, rows, depth)
    first, last = HALO, HALO + planes - 1
    group, row = walls.group, walls.row
    ones = jnp.ones((rows, depth), jnp.float32)
    zeros = jnp.zeros((rows, depth), jnp.float32)
    for d in range(HALO):
        for side, recv, x, there in (
            (1, end_ref, first - 1 - d, group > 0),
            (0, begin_ref, last + 1 + d, group < walls.groups - 1),
        ):
            side_r, side_source, own_source = ones, zeros, zeros
            if d < HALO - 1:
                at = (HALO - 1) * side + d
                near, far = near_ref[planes + at], corner_ref[at]
                side_r, side_source = halo_rows(near, far, walls.core, walls.tile, walls.tiles)
                own_source = recv[4 + d]
            rr_ref[x, 0:rows] = jnp.where(there, recv[d], 1.0)
            rr_ref[x, rows:ROWS] = jnp.where(there, side_r, 1.0)
            ss_ref[x, 0:rows] = jnp.where(there, own_source, 0.0)
            ss_ref[x, rows:ROWS] = jnp.where(there, side_source, 0.0)

    refs = tx_ref, ty_ref, tz_ref, w_ref, ws_ref
    for begin, end in ((1, first), (last, wide - 2)):
        before = tx_ref[last - 1] if begin == last else 2.0 / (rr_ref[0] + rr_ref[1])
        for x in range(begin, end + 1):
            wall = {first - 1: group == 0, last: group == walls.groups - 1}.get(x)
            before = walls.faces(storage, x, before, rr_ref, ss_ref, refs, wall)

    total = part_ref[0:rows]
    y_flux = part_ref[rows : rows + ROWS]
    link_y = part_ref[rows + ROWS :]
    for begin, end in ((2, first + 1), (last - 1, wide - 3)):
        before = start_flow(tx_ref, ws_ref, begin - 1)
        for x in range(begin, end + 1):
            ty = ty_ref[x]
            v, before = relax(
                ws_ref[x], ws_ref[x + 1], before, tx_ref[x], ty, tz_ref[x], w_ref[x], ws_ref[x], depth
            )
            v_ref[x] = v
            if first <= x <= last:
                total = total + ss_ref[x, 0:rows] - storage * v[0:rows]
                y_flux = y_flux + ty * (v - pltpu.roll(v, ROWS - 1, 0))
                link_y = link_y + ty[0:rows]

    out_left = tx_ref[first - 1, 0:rows] * (v_ref[first, 0:rows] - v_ref[first - 1, 0:rows])
    out_right = tx_ref[last, 0:rows] * (v_ref[last, 0:rows] - v_ref[last + 1, 0:rows])
    side = jnp.where(row == ROWS - 1, y_flux, jnp.where(row == rows - 1, -y_flux, 0.0))
    rhs = total - out_left - out_right + side[0:rows] + side[rows:ROWS]
    rhs = jnp.sum(rhs, keepdims=True)
    link_x = jnp.sum(tx_ref[last, 0:rows], keepdims=True)
    link_y = jnp.sum(jnp.where(row[0:rows] == rows - 1, link_y, 0.0), keepdims=True)
    lane = lax.broadcasted_iota(jnp.int32, (1, 128), 1) - (32 * group + 4 * walls.y)
    packed = jnp.where(lane == 0, rhs, 0.0) + jnp.where(lane == 1, link_x, 0.0)
    packed = packed + jnp.where(lane == 2, link_y, 0.0)
    for peer in range(sums_ref.shape[0]):
        sums_ref[peer] = packed


def relax(h, h_next, before, tx, ty, tz, w, ws, depth):
    ahead = tx * h
    flow = before + tx * h_next
    flow = flow + ty * pltpu.roll(h, h.shape[0] - 1, 0) + pltpu.roll(ty * h, 1, 0)
    flow = flow + tz * pltpu.roll(h, depth - 1, 1) + pltpu.roll(tz * h, 1, 1)
    return (1.0 - RELAX) * h + ws + w * flow, ahead


def merge_kernel(part_ref, out_ref):
    total = part_ref[0]
    for peer in range(1, part_ref.shape[0]):
        total = total + part_ref[peer]
    for peer in range(out_ref.shape[0]):
        out_ref[peer] = total


def before_by(pair, stride):
    even, odd = pair
    length = even.shape[0]
    if stride == 1:
        return pltpu.roll(odd, 1, 0), even
    shift = stride // 2
    return pltpu.roll(even, shift, 0), pltpu.roll(odd, shift, 0)


def after_by(pair, stride):
    even, odd = pair
    length = even.shape[0]
    if stride == 1:
        return odd, pltpu.roll(even, length - 1, 0)
    shift = length - stride // 2
    return pltpu.roll(even, shift, 0), pltpu.roll(odd, shift, 0)


def each(fn, *pairs):
    return tuple(fn(*values) for values in zip(*pairs, strict=True))


def coarse_solve(sums_ref, store_brick, levels):
    lines = sums_ref.shape[0] // 2
    lanes = sums_ref.shape[2]
    y_lane = lax.broadcasted_iota(jnp.int32, (8, lanes), 1) // 4 % 8
    own_y = y_lane == lax.broadcasted_iota(jnp.int32, (8, lanes), 0)

    def unpack(line):
        line = jnp.where(own_y, jnp.broadcast_to(line, (8, lanes)), 0.0)
        for shift in (16, 8, 4):
            line = line + pltpu.roll(line, lanes - shift, 1)
        return line

    rhs = tuple(
        jnp.concatenate([unpack(sums_ref[2 * z + core]) for z in range(lines)], axis=0)
        for core in range(2)
    )
    link_x = each(lambda a: pltpu.roll(a, lanes - 1, 1), rhs)
    link_y = each(lambda a: pltpu.roll(a, lanes - 2, 1), rhs)
    link_x_before = each(lambda a: pltpu.roll(a, 32, 1), link_x)
    link_y_before = before_by(link_y, 1)
    diagonal = each(lambda a, b, c, d: store_brick + a + b + c + d, link_x, link_x_before, link_y, link_y_before)
    upper = each(lambda a: -a, link_y)
    alphas, gammas = [], []
    for level in range(levels):
        stride = 1 << level
        inverse = each(lambda d: 1.0 / d, diagonal)
        ratio = each(lambda u, i: -u * i, upper, inverse)
        alpha = before_by(ratio, stride)
        gamma = each(lambda u, i: -u * i, upper, after_by(inverse, stride))
        low = before_by(each(lambda q, u: q * u, ratio, upper), stride)
        diagonal = each(lambda d, a, g, u: d + a + g * u, diagonal, low, gamma, upper)
        upper = each(lambda g, u: g * u, gamma, after_by(upper, stride))
        alphas.append(alpha)
        gammas.append(gamma)
    inverse = each(lambda d: 1.0 / d, diagonal)
    correction = None
    for sweep_no in range(COARSE_ITERS):
        now = rhs
        if sweep_no:
            now = each(
                lambda r, a, b, c: r + a * pltpu.roll(c, 32, 1) + b * pltpu.roll(c, lanes - 32, 1),
                rhs, link_x_before, link_x, correction,
            )
        for level in range(levels):
            stride = 1 << level
            now = each(
                lambda n, a, p, g, q: n + a * p + g * q,
                now, alphas[level], before_by(now, stride), gammas[level], after_by(now, stride),
            )
        correction = each(lambda n, i: n * i, now, inverse)
    return correction


def last_kernel(
    store_brick, levels, chunks,
    sums_ref, v_ref, tx_ref, ty_ref, tz_ref, w_ref, ws_ref,
    out_ref,
    lines_ref, g_ref, done_ref, sems,
):
    group, tile, core, _ = position()
    planes, rows, depth = out_ref.shape
    even, odd = coarse_solve(sums_ref, store_brick, levels)
    length = even.shape[0]
    for parity, line in ((0, even), (1, odd)):
        lines_ref[parity, 0:8] = jnp.zeros((8, line.shape[1]), jnp.float32)
        lines_ref[parity, 8 : 8 + length] = line
        lines_ref[parity, 8 + length : 16 + length] = jnp.zeros((8, line.shape[1]), jnp.float32)
    half = tile // 2
    here = lines_ref[core, pl.ds(8 + half, 1), :]
    ahead = lines_ref[1 - core, pl.ds(8 + half + core, 1), :]
    behind = lines_ref[1 - core, pl.ds(7 + half + core, 1), :]
    lane = lax.broadcasted_iota(jnp.int32, here.shape, 1)
    row = lax.broadcasted_iota(jnp.int32, (ROWS, depth), 0)

    def shift_of(offset):
        own, up, down = (
            jnp.sum(jnp.where(lane == 32 * (group + offset), line, 0.0), keepdims=True)
            for line in (here, ahead, behind)
        )
        return jnp.where(row < rows, own, jnp.where(row < rows + HALO, up, down))

    shifts = [shift_of(offset) for offset in (-1, 0, 1)]
    first, end = HALO, HALO + planes

    def third(x, h, h_next, before):
        v, ahead = relax(h, h_next, before, tx_ref[x], ty_ref[x], tz_ref[x], w_ref[x], ws_ref[x], depth)
        g_ref[x] = v
        return ahead

    def third_inside(x, carry):
        h, before = carry
        h_next = v_ref[x + 1] + shifts[1]
        return h_next, third(x, h, h_next, before)

    h = v_ref[first - 1] + shifts[0]
    h_next = v_ref[first] + shifts[1]
    before = third(first - 1, h, h_next, tx_ref[first - 2] * (v_ref[first - 2] + shifts[0]))
    h, before = lax.fori_loop(first, end - 1, third_inside, (h_next, before), unroll=31)
    h_next = v_ref[end] + shifts[2]
    before = third(end - 1, h, h_next, before)
    third(end, h_next, v_ref[end + 1] + shifts[2], before)

    def fourth(x, before):
        h = g_ref[x]
        h_own = h[0:rows]
        tx = tx_ref[x, 0:rows]
        tz = tz_ref[x, 0:rows]
        ty = ty_ref[x]
        ahead = tx * h_own
        flow = before + tx * g_ref[x + 1, 0:rows]
        flow = flow + (ty * pltpu.roll(h, ROWS - 1, 0) + pltpu.roll(ty * h, 1, 0))[0:rows]
        flow = flow + tz * pltpu.roll(h_own, depth - 1, 1) + pltpu.roll(tz * h_own, 1, 1)
        done_ref[x - HALO] = (1.0 - RELAX) * h_own + ws_ref[x, 0:rows] + w_ref[x, 0:rows] * flow
        return ahead

    before = tx_ref[first - 1, 0:rows] * g_ref[first - 1, 0:rows]
    step = planes // chunks
    copies = []
    for chunk in range(chunks):
        begin = first + chunk * step
        before = lax.fori_loop(begin, begin + step, fourth, before, unroll=16)
        part = pl.ds(chunk * step, step)
        copies.append(pltpu.make_async_copy(done_ref.at[part], out_ref.at[part], sems.at[chunk]))
        copies[-1].start()
    for copy in copies:
        copy.wait()


def spread(block, axes):
    return lax.all_to_all(block, axes, 0, 0)


def on_device(facies, perm_table, source):
    planes, rows, depth = source.shape
    storage = 0.01 / rows
    groups = lax.axis_size("group")
    z_size, y_size, cores = (lax.axis_size(a) for a in TILE_AXES)
    tiles = z_size * y_size * cores
    brick = f32(planes, rows, depth)
    chunks = 4
    r, source, near, far = call(
        functools.partial(rows_kernel, chunks),
        (brick, brick, f32(planes + 2 * (HALO - 1), rows, depth), f32(planes + 4 * HALO, rows, depth)),
        [HBM] * 3,
        [
            pltpu.SMEM(perm_table.shape, jnp.float32),
            pltpu.VMEM(source.shape, jnp.int32),
            pltpu.SemaphoreType.DMA,
            pltpu.SemaphoreType.DMA((2, chunks)),
        ],
        name="rows",
    )(*(pltpu.with_memory_space_constraint(a, pltpu.HBM) for a in (perm_table, facies, source)))
    pairs = [p for i in range(1, tiles - 1, 2) for p in ((i, i + 1), (i + 1, i))]
    far = lax.ppermute(far, TILE_AXES, pairs)
    slab = f32(7, rows, depth)
    begin, end = call(planes_kernel, (slab, slab), [VMEM] * 2, name="planes")(r, source)
    end = lax.ppermute(end, "group", [(i, i + 1) for i in range(groups - 1)])
    begin = lax.ppermute(begin, "group", [(i + 1, i) for i in range(groups - 1)])
    wide = f32(planes + 2 * HALO, ROWS, depth)
    tx, tz, w = call(functools.partial(own_kernel, storage), (wide,) * 3, [VMEM], name="own")(r)
    near, tx, tz, w = lax.optimization_barrier((near, tx, tz, w))
    near, corner = call(
        corners_kernel,
        (f32(*near.shape), f32(2 * (HALO - 1), rows, depth)),
        [VMEM] * 3,
        name="corners",
        aliases={2: 0},
    )(begin, end, near)
    near = lax.ppermute(near, "core", [(0, 1), (1, 0)])
    corner = lax.ppermute(corner, TILE_AXES, pairs)
    part, *fields = call(
        functools.partial(middle_kernel, storage),
        (f32(2 * rows + ROWS, depth),) + (wide,) * 8,
        [VMEM] * 7,
        name="middle",
        aliases={4: 2, 5: 4, 6: 5},
    )(r, source, near, far, tx, tz, w)
    sums, *fields = call(
        functools.partial(edges_kernel, storage),
        (f32(groups * y_size, 1, 128),) + (wide,) * 8,
        [VMEM] * 13,
        name="edges",
        aliases={5 + i: 1 + i for i in range(8)},
    )(begin, end, near, corner, part, *fields)
    fields = fields[:6]
    sums = spread(sums, ("group", "y"))
    sums = call(merge_kernel, f32(z_size * cores, 1, 128), [VMEM], name="merge")(sums)
    sums = spread(sums, ("z", "core"))
    length = z_size * y_size
    chunks = 4
    return call(
        functools.partial(last_kernel, storage * planes * rows * depth, tiles.bit_length() - 1, chunks),
        brick,
        [VMEM] * 7,
        [
            pltpu.VMEM((2, length + 16, 128), jnp.float32),
            pltpu.VMEM(wide.shape, jnp.float32),
            pltpu.VMEM(brick.shape, jnp.float32),
            pltpu.SemaphoreType.DMA((chunks,)),
        ],
        name="last",
        out_spec=HBM,
    )(sums, *fields)


def solution(mesh):
    groups, tiles = mesh.shape["group"], mesh.shape["tile"]
    chips = Mesh(mesh.devices.reshape(groups, tiles // 16, 8, 2), ("group",) + TILE_AXES)
    cells = P("group", TILE_AXES, None)
    return jax.shard_map(
        on_device, mesh=chips, in_specs=(cells, P(), cells), out_specs=cells, check_vma=False
    )
```
